32 devices in a mesh: orb: 16 (over z, y, core), fft: 2 (over x).
Axes of the slice: x: 2, y: 2, z: 4, core: 2. Of those that a mesh axis runs over, the one named last changes fastest.
Arguments:
- orbitals: bfloat16 [128, 256, 256], P('orb', 'fft'), may hold values from -6 to 6
- kernel: float32 [256, 256], P('fft'), may hold values from 0.02 to 2
- partner_owner: int32 [128, 2, 1], P('orb'), may hold values from 0 to 15; in each aligned block of 16 rows (0 to 15, 16 to 31, ..., all dimensions but the last counted through in order) at most 2 rows name the same one
- partner_local: int32 [128, 2], P('orb'), may hold values from 0 to 7
Outputs:
- exchange_term: float32 [128, 256, 256], P('orb', 'fft')
The draws below stay inside these ranges and needn't reach their ends.
Inputs may be any that keep to these rules, and one draw needn't show every extreme that they name: `partner_owner`: among the 16 partners named on one index of orb, no owner is named more than 2 times, a bound that some block reaches; every owner is named somewhere.
All inputs are finite; a program needn't handle non-finite values.
Results may differ from the reference program's by a relative error of at most 0.0004.
Values may be sent and summed in bfloat16 or wider, within the bound.
A program may use at most 64 MiB of HBM per device.

```python
import math
import jax
import jax.numpy as jnp
import numpy as np
from jax import lax

GX = 256
GY = 256
ORB_DEV = 8
TASK_DEV = 8
CAP = 2
NORB = 128
TASKS = 128
N_ORB = 16


def place_ends(entries, key, smallest, largest):
    index_at = [jax.random.randint(jax.random.fold_in(key, axis), (), 0, length) for axis, length in enumerate(entries.shape)]
    widest = entries.shape.index(max(entries.shape))
    next_to = index_at[:widest] + [(index_at[widest] + 1) % entries.shape[widest]] + index_at[widest + 1:]
    return entries.at[tuple(index_at)].set(smallest).at[tuple(next_to)].set(largest)


def levels(own_key, dims, cuts, least, largest):
    def one(axis_at, parts):
        draws = jax.random.uniform(jax.random.fold_in(jax.random.fold_in(own_key, 6), axis_at), (parts,), jnp.float32, least / len(cuts), largest / len(cuts))
        return jnp.repeat(jnp.exp(draws), dims[axis_at] // parts).reshape((-1,) + (1,) * (len(dims) - axis_at - 1))

    factor_of = one(*cuts[0])
    for cut in cuts[1:]:
        factor_of = factor_of * one(*cut)
    return factor_of


def routed_block(stream_key, own, number, rows, count, top, bound, slope):
    ranking = jax.random.permutation(stream_key, count)
    packed, usual = load_shares(count, rows * top, bound, slope, True), load_shares(count, rows * top, bound, slope, False)
    places = jnp.arange(count)

    def named(lengths, offset_by):
        used = int((lengths > 0).sum())
        fixed = max(1, used // 4)
        moved = fixed + (places - fixed + offset_by * (used - fixed)) % max(1, count - fixed)
        return jnp.zeros((count,), jnp.int32).at[ranking[jnp.where(places < fixed, places, moved)]].set(jnp.asarray(lengths, jnp.int32))

    lengths = jnp.where(number % 4 == 0, named(packed, number // 4), named(usual, number - number // 4 - 1))
    mixed = jax.random.permutation(jax.random.fold_in(own, 3), count)
    source_of, sink = mixed[0:count // 2 * 2:2], mixed[1:count // 2 * 2:2]
    margin = jnp.minimum(lengths[source_of] - 1, bound - lengths[sink]) // 2
    margin = jnp.where((source_of == ranking[0]) | (sink == ranking[0]) | (lengths[sink] == 0), 0, jnp.maximum(margin, 0))
    moved = jax.random.randint(jax.random.fold_in(own, 4), (count // 2,), 0, 1 << 20) % (margin + 1)
    lengths = lengths.at[source_of].add(-moved).at[sink].add(moved)
    labels = jnp.searchsorted(jnp.cumsum(lengths), jnp.arange(rows * top), side="right").astype(jnp.int32)
    listing = labels.reshape(top, rows).T
    listing = listing[jax.random.permutation(jax.random.fold_in(own, 1), rows)]
    offset_by = jax.random.randint(jax.random.fold_in(own, 2), (rows, 1), 0, top)
    return jnp.take_along_axis(listing, (jnp.arange(top)[None, :] + offset_by) % top, axis=1)


def load_shares(number_of, total, limit, slope, full):
    portions = [(1 << 20) // math.isqrt(standing ** slope) + 1 for standing in range(1, number_of + 1)]
    largest = limit if full else min(limit, max(-(-total // number_of), total * portions[0] // sum(portions)))
    least = 1 if total - largest >= number_of - 1 else 0
    given, spare = [largest] + [least] * (number_of - 1), total - largest - least * (number_of - 1)
    while spare > 0:
        free = [i for i in range(1, number_of) if given[i] < largest] or [i for i in range(1, number_of) if given[i] < limit]
        mass, budget = sum([portions[i] for i in free]), spare
        for i in free:
            extra = min(limit - given[i], max(1, budget * portions[i] // mass), spare)
            given[i] = given[i] + extra
            spare = spare - extra
    return np.array(given)


def centred(own_key, dims, deviation, reach, split=(), dtype=jnp.bfloat16):
    result = deviation * jax.random.normal(own_key, dims, jnp.float32)
    if split:
        result = result * levels(own_key, dims, split, -0.22, 0.18)
    return jnp.clip(result, -reach, reach).astype(dtype)


def setup_inputs(seed: int = 0) -> dict:
    arg_keys = jax.random.split(jax.random.key(seed), 5)
    orbitals = centred(arg_keys[0], (NORB, GX, GY), 1.0, 6.0, ((0, 16), (1, 2)))
    kernel = jnp.clip(jnp.exp(math.log(2.0) - 4.6051702 * jax.random.uniform(arg_keys[1], (GY, GX), jnp.float32) ** levels(arg_keys[1], (GY, GX), ((0, 2),), -0.2, 0.2)), 0.02, 2.0)
    partner_owner_keys = jax.random.split(jax.random.fold_in(arg_keys[2], 1), TASKS * 2 // (2 * TASK_DEV))
    partner_owner_turns = jax.random.permutation(jax.random.fold_in(arg_keys[2], 3), TASKS * 2 // (2 * TASK_DEV))
    partner_owner = jax.vmap(lambda own, number: routed_block(jax.random.fold_in(arg_keys[2], 2), own, number, 2 * TASK_DEV, N_ORB, 1, CAP, 2))(partner_owner_keys, partner_owner_turns).reshape((TASKS, 2, 1))
    partner_local = place_ends(jax.random.randint(arg_keys[3], (TASKS, 2), 0, ORB_DEV), jax.random.fold_in(arg_keys[3], 1), 0, ORB_DEV - 1).astype(jnp.int32)
    return dict(orbitals=orbitals, kernel=kernel, partner_owner=partner_owner, partner_local=partner_local)


def reference(orbitals, kernel, partner_owner, partner_local):
    pair_ids = (partner_owner[:, :, 0] * ORB_DEV + partner_local).astype(jnp.int32)
    blocks = pair_ids.reshape(N_ORB, TASK_DEV, 2)
    weight = kernel.T.astype(jnp.float32)

    def step(total, block):
        first = orbitals[block[:, 0]].astype(jnp.float32)
        second = orbitals[block[:, 1]].astype(jnp.float32)
        density = first * second
        spectrum = jnp.fft.fft2(density, axes=(1, 2))
        potential = jnp.real(jnp.fft.ifft2(spectrum * weight[None], axes=(1, 2))).astype(jnp.float32)
        total = total.at[block[:, 0]].add(potential * second)
        total = total.at[block[:, 1]].add(potential * first)
        return total, None

    start = jnp.zeros((NORB, GX, GY), jnp.float32)
    total, unused = lax.scan(step, start, blocks)
    return -total
```

```python
import math

import jax
import jax.numpy as jnp
import numpy as np
from jax import lax
from jax.sharding import PartitionSpec as P

LEVELS = 32767.0
STEPS = 128.0
LANES = 128


def angles(length):
    series = np.arange(length)
    return (series[:, None] * series[None, :] % length) * (2.0 * math.pi / length)


def packed_tables(length):
    half = length // 2
    angle = angles(length)[:, :half]
    sine = np.sin(angle)
    sine[:, 0] = np.cos(math.pi * np.arange(length))
    forward = np.concatenate([np.cos(angle), sine], axis=1)
    gain = np.full((2 * half,), 2.0)
    gain[0] = gain[half] = 1.0
    backward = (forward * gain).T
    return forward.astype(np.float32), backward.astype(np.float32)


def product(form, left, right):
    return jnp.einsum(form, left, right, precision=lax.Precision.HIGH, preferred_element_type=jnp.float32)


def weights(kernel):
    half = kernel.shape[0] // 2
    mirror = jnp.roll(jnp.flip(kernel, (0, 1)), 1, (0, 1))
    even = (0.5 * (kernel + mirror)).T
    plus = even[:, :half]
    minus = jnp.concatenate([even[:, half : half + 1], even[:, 1:half]], axis=1)
    return plus, minus


def convolve(density, kernel):
    full_x, width_y = density.shape[1:]
    half = width_y // 2
    forward, backward = packed_tables(width_y)
    angle = angles(full_x)
    both = np.concatenate([np.cos(angle), np.sin(angle)], axis=0).astype(np.float32)
    plus, minus = weights(kernel)
    scale = 1.0 / (full_x * width_y)
    weight = jnp.concatenate([plus, minus], axis=1) * scale
    spread = product("txy,yk->txk", density, forward)
    mixed = product("qx,txk->tqk", both, spread)
    cos_part = mixed[:, :full_x] * weight
    sin_part = mixed[:, full_x:] * weight
    first = cos_part[:, :, :half] - sin_part[:, :, half:]
    second = sin_part[:, :, :half] + cos_part[:, :, half:]
    back = product("qx,txk->tqk", both, jnp.concatenate([first, second], axis=2))
    cos_part = back[:, :full_x]
    sin_part = back[:, full_x:]
    real = cos_part[:, :, :half] + sin_part[:, :, half:]
    imag = cos_part[:, :, half:] - sin_part[:, :, :half]
    return product("txk,ky->txy", jnp.concatenate([real, imag], axis=2), backward)


def encode(values, run):
    rows, width = values.shape
    runs = values.reshape(rows, width // run, run)
    peak = jnp.maximum(jnp.max(jnp.abs(runs), axis=2), 1e-30)
    level = jnp.ceil(jnp.log2(peak) * STEPS + 0.01)
    rate = jnp.exp2(level / STEPS)
    coded = jnp.round(runs * (LEVELS / rate)[:, :, None]).reshape(rows, width)
    extra = jnp.pad(level, ((0, 0), (0, LANES - width // run)))
    return jnp.concatenate([coded, extra], axis=1).astype(jnp.int16)


def decode(coded, run):
    rows = coded.shape[0]
    width = coded.shape[1] - LANES
    level = coded[:, width : width + width // run].astype(jnp.float32)
    rate = jnp.exp2(level / STEPS) / LEVELS
    runs = coded[:, :width].astype(jnp.float32).reshape(rows, width // run, run)
    return (runs * rate[:, :, None]).reshape(rows, width)


def on_device(orbitals, kernel, partner_owner, partner_local):
    peers = lax.axis_size("orb")
    parts = lax.axis_size("fft")
    orb_dev, rows_x, width_y = orbitals.shape
    tasks_dev = partner_local.shape[0]
    tasks = tasks_dev * peers
    norb = orb_dev * peers
    full_x = rows_x * parts
    chunk = rows_x * width_y // peers
    run = min(width_y, chunk)
    own = tasks // (peers * parts)

    whole = lax.all_to_all(
        jnp.broadcast_to(kernel[None], (parts,) + kernel.shape), "fft", 0, 0, tiled=True
    ).reshape(parts * kernel.shape[0], kernel.shape[1])
    named = partner_owner[:, :, 0] * orb_dev + partner_local
    named = jnp.broadcast_to(named[None], (peers, tasks_dev, 2))
    pair_ids = lax.all_to_all(named, "orb", 0, 0, tiled=True).reshape(tasks, 2)
    held = lax.all_to_all(
        orbitals.reshape(orb_dev, peers, chunk).transpose(1, 0, 2), "orb", 0, 0, tiled=True
    ).reshape(norb, chunk)

    pick = (pair_ids.T.reshape(2 * tasks, 1) == jnp.arange(norb, dtype=jnp.int32)[None, :]).astype(jnp.bfloat16)
    chosen = jnp.dot(pick, held, preferred_element_type=jnp.float32)
    first, second = chosen[:tasks], chosen[tasks:]
    density = first * second

    sent = encode(density, run).reshape(parts, peers, own, chunk + LANES)
    got = lax.all_to_all(sent.reshape(parts * peers * own, chunk + LANES), ("fft", "orb"), 0, 0, tiled=True)
    grid = decode(got, run).reshape(parts * peers, own, chunk)
    grid = grid.transpose(1, 0, 2).reshape(own, full_x, width_y)
    potential = convolve(grid, whole)
    potential = potential.reshape(own, parts * peers, chunk).transpose(1, 0, 2)
    sent = encode(potential.reshape(parts * peers * own, chunk), run)
    got = lax.all_to_all(sent, ("fft", "orb"), 0, 0, tiled=True)
    potential = decode(got, run)

    terms = jnp.concatenate([potential * second, potential * first], axis=0)
    high = lax.reduce_precision(terms, 8, 7)
    low = (terms - high).astype(jnp.bfloat16)
    high = high.astype(jnp.bfloat16)
    total = jnp.einsum(
        "to,tc->oc",
        jnp.concatenate([pick, pick], axis=0),
        jnp.concatenate([high, low], axis=0),
        preferred_element_type=jnp.float32,
    )
    sent = encode(-total, run)
    got = decode(lax.all_to_all(sent, "orb", 0, 0, tiled=True), run)
    return got.reshape(peers, orb_dev, chunk).transpose(1, 0, 2).reshape(orb_dev, rows_x, width_y)


def solution(mesh):
    in_specs = (P("orb", "fft", None), P("fft", None), P("orb", None, None), P("orb", None))
    out_specs = P("orb", "fft", None)
    return jax.shard_map(
        on_device, mesh=mesh, in_specs=in_specs, out_specs=out_specs, check_vma=False
    )
```

```python
import functools
import math

import jax
import jax.numpy as jnp
import numpy as np
from jax import lax
from jax.experimental import pallas as pl
from jax.experimental.pallas import tpu as pltpu
from jax.sharding import PartitionSpec as P

LEVELS = 32767.0
STEPS = 128.0
LANES = 128


def angles(length):
    series = np.arange(length)
    return (series[:, None] * series[None, :] % length) * (2.0 * math.pi / length)


def packed_tables(length):
    half = length // 2
    angle = angles(length)[:, :half]
    sine = np.sin(angle)
    sine[:, 0] = np.cos(math.pi * np.arange(length))
    forward = np.concatenate([np.cos(angle), sine], axis=1)
    gain = np.full((2 * half,), 2.0)
    gain[0] = gain[half] = 1.0
    backward = (forward * gain).T
    return forward.astype(np.float32), backward.astype(np.float32)


def product(form, left, right):
    return jnp.einsum(form, left, right, precision=lax.Precision.HIGH, preferred_element_type=jnp.float32)


def weights(kernel):
    half = kernel.shape[0] // 2
    mirror = jnp.roll(jnp.flip(kernel, (0, 1)), 1, (0, 1))
    even = (0.5 * (kernel + mirror)).T
    plus = even[:, :half]
    minus = jnp.concatenate([even[:, half : half + 1], even[:, 1:half]], axis=1)
    return plus, minus


def convolve(density, kernel):
    full_x, width_y = density.shape[1:]
    half = width_y // 2
    forward, backward = packed_tables(width_y)
    angle = angles(full_x)
    both = np.concatenate([np.cos(angle), np.sin(angle)], axis=0).astype(np.float32)
    plus, minus = weights(kernel)
    scale = 1.0 / (full_x * width_y)
    weight = jnp.concatenate([plus, minus], axis=1) * scale
    spread = product("txy,yk->txk", density, forward)
    mixed = product("qx,txk->tqk", both, spread)
    cos_part = mixed[:, :full_x] * weight
    sin_part = mixed[:, full_x:] * weight
    first = cos_part[:, :, :half] - sin_part[:, :, half:]
    second = sin_part[:, :, :half] + cos_part[:, :, half:]
    back = product("qx,txk->tqk", both, jnp.concatenate([first, second], axis=2))
    cos_part = back[:, :full_x]
    sin_part = back[:, full_x:]
    real = cos_part[:, :, :half] + sin_part[:, :, half:]
    imag = cos_part[:, :, half:] - sin_part[:, :, :half]
    return product("txk,ky->txy", jnp.concatenate([real, imag], axis=2), backward)


def encode(values, run):
    rows, width = values.shape
    runs = values.reshape(rows, width // run, run)
    peak = jnp.maximum(jnp.max(jnp.abs(runs), axis=2), 1e-30)
    level = jnp.ceil(jnp.log2(peak) * STEPS + 0.01)
    rate = jnp.exp2(level / STEPS)
    coded = jnp.round(runs * (LEVELS / rate)[:, :, None]).reshape(rows, width)
    extra = jnp.pad(level, ((0, 0), (0, LANES - width // run)))
    return jnp.concatenate([coded, extra], axis=1).astype(jnp.int16)


def decode(coded, run):
    rows = coded.shape[0]
    width = coded.shape[1] - LANES
    level = coded[:, width : width + width // run].astype(jnp.float32)
    rate = jnp.exp2(level / STEPS) / LEVELS
    runs = coded[:, :width].astype(jnp.float32).reshape(rows, width // run, run)
    return (runs * rate[:, :, None]).reshape(rows, width)


def plain_device(orbitals, kernel, partner_owner, partner_local):
    peers = lax.axis_size("orb")
    parts = lax.axis_size("fft")
    orb_dev, rows_x, width_y = orbitals.shape
    tasks_dev = partner_local.shape[0]
    tasks = tasks_dev * peers
    norb = orb_dev * peers
    full_x = rows_x * parts
    chunk = rows_x * width_y // peers
    run = min(width_y, chunk)
    own = tasks // (peers * parts)

    whole = lax.all_to_all(
        jnp.broadcast_to(kernel[None], (parts,) + kernel.shape), "fft", 0, 0, tiled=True
    ).reshape(parts * kernel.shape[0], kernel.shape[1])
    named = partner_owner[:, :, 0] * orb_dev + partner_local
    named = jnp.broadcast_to(named[None], (peers, tasks_dev, 2))
    pair_ids = lax.all_to_all(named, "orb", 0, 0, tiled=True).reshape(tasks, 2)
    held = lax.all_to_all(
        orbitals.reshape(orb_dev, peers, chunk).transpose(1, 0, 2), "orb", 0, 0, tiled=True
    ).reshape(norb, chunk)

    pick = (pair_ids.T.reshape(2 * tasks, 1) == jnp.arange(norb, dtype=jnp.int32)[None, :]).astype(jnp.bfloat16)
    chosen = jnp.dot(pick, held, preferred_element_type=jnp.float32)
    first, second = chosen[:tasks], chosen[tasks:]
    density = first * second

    sent = encode(density, run).reshape(parts, peers, own, chunk + LANES)
    got = lax.all_to_all(sent.reshape(parts * peers * own, chunk + LANES), ("fft", "orb"), 0, 0, tiled=True)
    grid = decode(got, run).reshape(parts * peers, own, chunk)
    grid = grid.transpose(1, 0, 2).reshape(own, full_x, width_y)
    potential = convolve(grid, whole)
    potential = potential.reshape(own, parts * peers, chunk).transpose(1, 0, 2)
    sent = encode(potential.reshape(parts * peers * own, chunk), run)
    got = lax.all_to_all(sent, ("fft", "orb"), 0, 0, tiled=True)
    potential = decode(got, run)

    terms = jnp.concatenate([potential * second, potential * first], axis=0)
    high = lax.reduce_precision(terms, 8, 7)
    low = (terms - high).astype(jnp.bfloat16)
    high = high.astype(jnp.bfloat16)
    total = jnp.einsum(
        "to,tc->oc",
        jnp.concatenate([pick, pick], axis=0),
        jnp.concatenate([high, low], axis=0),
        preferred_element_type=jnp.float32,
    )
    sent = encode(-total, run)
    got = decode(lax.all_to_all(sent, "orb", 0, 0, tiled=True), run)
    return got.reshape(peers, orb_dev, chunk).transpose(1, 0, 2).reshape(orb_dev, rows_x, width_y)


F32 = jnp.float32
BF16 = jnp.bfloat16
MESH = pl.DeviceIdType.MESH


def split(values):
    high = values.astype(BF16)
    return high, (values - high.astype(F32)).astype(BF16)


def dot(left, right):
    return jnp.dot(left, right, preferred_element_type=F32)


def left_table(table, values):
    high, low = split(values)
    return dot(table[0], high) + dot(table[0], low) + dot(table[1], high)


def right_table(values, table):
    high, low = split(values)
    return dot(high, table[0]) + dot(low, table[0]) + dot(high, table[1])


def iota(shape, axis):
    return lax.broadcasted_iota(jnp.int32, shape, axis)


def quantize(values, first_row=0):
    count, rows, _ = values.shape
    peak = jnp.maximum(jnp.max(jnp.abs(values), axis=2, keepdims=True), 1e-30)
    coded = jnp.round(values * (LEVELS / peak)).astype(jnp.int32).astype(jnp.int16)
    shape = (count, rows, LANES)
    spot = iota(shape, 2) == iota(shape, 1) + first_row
    scale = jnp.sum(jnp.where(spot, peak * (1.0 / LEVELS), 0.0), axis=1, keepdims=True)
    return coded, scale


def restore(coded, scale, first_row=0):
    count, rows, _ = coded.shape
    shape = (count, rows, LANES)
    spot = iota(shape, 2) == iota(shape, 1) + first_row
    rate = jnp.sum(jnp.where(spot, jnp.broadcast_to(scale, shape), 0.0), axis=2, keepdims=True)
    return coded.astype(jnp.int32).astype(F32) * rate


def half_roll(values):
    parts = [
        pltpu.roll(values[:, at : at + LANES], LANES // 2, 1) for at in range(0, values.shape[1], LANES)
    ]
    return jnp.concatenate(parts, axis=1)


def fused(
    peers, parts, rows, orb_dev, task_dev,
    orb_ref, ids_ref, ker_ref, fwd_ref, bwd_ref, both_ref, out_ref,
    held, names, whole, chosen, snd1, rec1, sc_snd1, sc_rec1, snd2, rec2, sc_snd2, sc_rec2,
    terms, snd3, rec3, sc_snd3, sc_rec3, send_sem, recv_sem,
):
    o = lax.axis_index("orb")
    f = lax.axis_index("fft")
    everyone = peers * parts
    me = f * peers + o
    block = task_dev * rows
    tasks = task_dev * peers
    width = orb_ref.shape[2]
    half = width // 2
    full_x = ker_ref.shape[2]

    barrier = pltpu.get_barrier_semaphore()

    def greet(i, c):
        p = lax.rem(me + i, everyone)
        pl.semaphore_signal(barrier, inc=1, device_id=(lax.rem(p, peers), p // peers), device_id_type=MESH)
        return c

    lax.fori_loop(1, everyone, greet, 0)
    pl.semaphore_wait(barrier, everyone - 1)

    def remote(src, dst, k, device):
        return pltpu.make_async_remote_copy(
            src_ref=src, dst_ref=dst, send_sem=send_sem.at[k], recv_sem=recv_sem.at[k],
            device_id=device, device_id_type=MESH,
        )

    def over_orb(src, dst, k, fixed=False):
        def one(i, c):
            p = lax.rem(o + i, peers)
            remote(src if fixed else src.at[p], dst.at[o], k, (p, f)).start()
            return c

        pltpu.make_async_copy(src if fixed else src.at[o], dst.at[o], recv_sem.at[k]).start()
        lax.fori_loop(1, peers, one, 0)

    def over_all(src, dst, k):
        def one(i, c):
            p = lax.rem(me + i, everyone)
            remote(src.at[p], dst.at[me], k, (lax.rem(p, peers), p // peers)).start()
            return c

        pltpu.make_async_copy(src.at[me], dst.at[me], recv_sem.at[k]).start()
        lax.fori_loop(1, everyone, one, 0)

    def arrived(dst, k):
        pltpu.make_async_copy(dst, dst, recv_sem.at[k]).wait()

    def left(dst, k):
        gone = dst.at[pl.ds(0, dst.shape[0] - 1)]
        pltpu.make_async_copy(gone, gone, send_sem.at[k]).wait()

    over_orb(ids_ref, names, 0, fixed=True)
    over_orb(orb_ref, held, 1)

    def halves(i, c):
        p = lax.rem(f + i, parts)
        remote(ker_ref.at[0], whole.at[f], 2, (o, p)).start()
        return c

    pltpu.make_async_copy(ker_ref.at[0], whole.at[f], recv_sem.at[2]).start()
    lax.fori_loop(1, parts, halves, 0)

    arrived(whole, 2)
    per = half // parts
    turned = split(whole[...].reshape(width, full_x).T)
    lane = iota((width, LANES), 1)
    freq = f * per + lax.rem(lane, per)
    freq = jnp.where((lane >= per) & (freq == 0), half, freq)
    row = iota((width, LANES), 0)
    straight = (row == freq).astype(F32).astype(BF16)
    mirror = (row == lax.rem(width - freq, width)).astype(F32).astype(BF16)
    flip_shape = (full_x, full_x)
    flip = (iota(flip_shape, 1) == lax.rem(full_x - iota(flip_shape, 0), full_x)).astype(F32).astype(BF16)
    plain = dot(turned[0], straight) + dot(turned[1], straight)
    other = split(dot(turned[0], mirror) + dot(turned[1], mirror))
    weight = (plain + dot(flip, other[0]) + dot(flip, other[1])) * (0.5 / (full_x * width))
    sign = jnp.where(iota((full_x, 2 * LANES), 1) % LANES < per, 1.0, -1.0)
    weight = jnp.concatenate([weight, weight], axis=1)
    signed = weight * sign

    arrived(names, 0)
    named = names[...].reshape(tasks, LANES)
    grow = (iota((tasks * rows, tasks), 0) // rows == iota((tasks * rows, tasks), 1)).astype(F32).astype(BF16)
    down = dot(grow, named.astype(BF16)).astype(jnp.int32) * rows + iota((tasks * rows, LANES), 0) % rows
    spread = (iota((tasks, tasks * rows), 1) // rows == iota((tasks, tasks * rows), 0)).astype(F32).astype(BF16)
    across = dot(named.T[:8].astype(BF16), spread).astype(jnp.int32) * rows + iota((8, tasks * rows), 1) % rows

    arrived(held, 1)
    total_rows = tasks * rows
    norb_rows = peers * orb_dev * rows
    step = 4 * block
    blocks = total_rows // step

    source = held[...].reshape(norb_rows, width)
    for b in range(blocks):
        at = slice(b * step, (b + 1) * step)
        pair = []
        for c in range(2):
            hot = (down[at, c : c + 1] == iota((step, norb_rows), 1)).astype(F32).astype(BF16)
            value = dot(hot, source)
            chosen[c, at, :] = value.astype(BF16)
            pair.append(value)
        waves = right_table(pair[0] * pair[1], fwd_ref)
        for h in range(parts):
            coded, scale = quantize(waves[:, h * LANES : (h + 1) * LANES].reshape(4, block, LANES))
            snd1[h * peers + 4 * b : h * peers + 4 * b + 4] = coded
            sc_snd1[h * peers + 4 * b : h * peers + 4 * b + 4] = scale
    over_all(sc_snd1, sc_rec1, 3)
    over_all(snd1, rec1, 4)

    arrived(sc_rec1, 3)
    arrived(rec1, 4)
    scales = sc_rec1[...]
    sent = jnp.zeros((everyone, 1, LANES), F32)
    for i in range(task_dev // 2):
        at = slice(2 * rows * i, 2 * rows * (i + 1))
        values = restore(rec1[:, at, :], scales, 2 * rows * i)
        grid = jnp.concatenate(
            [values[:, :rows].reshape(full_x, LANES), values[:, rows:].reshape(full_x, LANES)], axis=1
        )
        mixed = left_table(both_ref, grid)
        mixed = mixed[:full_x] * weight + half_roll(mixed[full_x:] * signed)
        mixed = left_table(both_ref, mixed)
        mixed = mixed[:full_x] + half_roll(mixed[full_x:]) * sign
        values = jnp.concatenate(
            [mixed[:, :LANES].reshape(everyone, rows, LANES), mixed[:, LANES:].reshape(everyone, rows, LANES)],
            axis=1,
        )
        coded, scale = quantize(values, 2 * rows * i)
        snd2[:, at, :] = coded
        sent = sent + scale
    sc_snd2[...] = sent
    over_all(sc_snd2, sc_rec2, 5)
    over_all(snd2, rec2, 6)

    arrived(sc_rec2, 5)
    arrived(rec2, 6)
    for b in range(blocks):
        at = slice(b * step, (b + 1) * step)
        waves = []
        for h in range(parts):
            spot = slice(h * peers + 4 * b, h * peers + 4 * b + 4)
            waves.append(restore(rec2[spot], sc_rec2[spot]).reshape(step, LANES))
        potential = right_table(jnp.concatenate(waves, axis=1), bwd_ref)
        for c in range(2):
            high, low = split(potential * chosen[1 - c, at, :].astype(F32))
            to = slice(c * total_rows + b * step, c * total_rows + (b + 1) * step)
            terms[0, to, :] = high
            terms[1, to, :] = low
    ids_row = jnp.concatenate([across[0:1], across[1:2]], axis=1)
    for b in range(norb_rows // step):
        hot = (ids_row == iota((step, 2 * total_rows), 0) + b * step).astype(F32).astype(BF16)
        total = -(dot(hot, terms[0]) + dot(hot, terms[1]))
        coded, scale = quantize(total.reshape(4, block, width))
        snd3[4 * b : 4 * b + 4] = coded
        sc_snd3[4 * b : 4 * b + 4] = scale
    over_orb(sc_snd3, sc_rec3, 7)
    over_orb(snd3, rec3, 8)
    arrived(sc_rec3, 7)
    arrived(rec3, 8)
    for p in range(peers):
        values = restore(rec3[p : p + 1], sc_rec3[p : p + 1]).reshape(orb_dev, rows, width)
        out_ref[:, p * rows : (p + 1) * rows, :] = values

    left(names, 0)
    left(held, 1)
    gone = whole.at[pl.ds(0, parts - 1)]
    pltpu.make_async_copy(gone, gone, send_sem.at[2]).wait()
    left(sc_snd1, 3)
    left(snd1, 4)
    left(sc_snd2, 5)
    left(snd2, 6)
    left(sc_snd3, 7)
    left(snd3, 8)


def tables_of(array):
    exact = jnp.asarray(array, F32)
    high = lax.reduce_precision(exact, 8, 7)
    return jnp.stack([high.astype(BF16), (exact - high).astype(BF16)])


def fused_device(orbitals, kernel, partner_owner, partner_local):
    peers = lax.axis_size("orb")
    parts = lax.axis_size("fft")
    orb_dev, rows_x, width = orbitals.shape
    task_dev = partner_local.shape[0]
    rows = rows_x // peers
    full_x = rows_x * parts
    everyone = peers * parts
    block = orb_dev * rows
    half = width // 2
    per = half // parts

    named = (partner_owner[:, :, 0] * orb_dev + partner_local).astype(F32)
    named = jnp.pad(named, ((0, 0), (0, LANES - 2)))
    sent = orbitals.reshape(orb_dev, peers, rows, width).transpose(1, 0, 2, 3).reshape(peers, block, width)
    forward, backward = packed_tables(width)
    order = np.concatenate(
        [np.concatenate([np.arange(h * per, (h + 1) * per), half + np.arange(h * per, (h + 1) * per)]) for h in range(parts)]
    )
    angle = angles(full_x)
    both = np.concatenate([np.cos(angle), np.sin(angle)], axis=0)
    vmem = pl.BlockSpec(memory_space=pltpu.VMEM)
    pieces = lambda n, w, t: [pltpu.VMEM((n, block, w), t), pltpu.VMEM((n, block, w), t)]
    rates = lambda n: [pltpu.VMEM((n, 1, LANES), F32), pltpu.VMEM((n, 1, LANES), F32)]
    rows_all = task_dev * peers * rows
    return pl.pallas_call(
        functools.partial(fused, peers, parts, rows, orb_dev, task_dev),
        out_shape=jax.ShapeDtypeStruct((orb_dev, rows_x, width), F32),
        in_specs=[vmem] * 6,
        out_specs=vmem,
        scratch_shapes=[
            pltpu.VMEM((peers, block, width), BF16),
            pltpu.VMEM((peers, task_dev, LANES), F32),
            pltpu.VMEM((parts,) + kernel.shape, F32),
            pltpu.VMEM((2, rows_all, width), BF16),
            *pieces(everyone, LANES, jnp.int16), *rates(everyone),
            *pieces(everyone, LANES, jnp.int16), *rates(everyone),
            pltpu.VMEM((2, 2 * rows_all, width), BF16),
            *pieces(peers, width, jnp.int16), *rates(peers),
            pltpu.SemaphoreType.DMA((9,)),
            pltpu.SemaphoreType.DMA((9,)),
        ],
        compiler_params=pltpu.CompilerParams(
            collective_id=0, has_side_effects=True, vmem_limit_bytes=60 * 1024 * 1024
        ),
    )(sent, named, kernel[None], tables_of(forward[:, order]), tables_of(backward[order]), tables_of(both))


def on_device(orbitals, kernel, partner_owner, partner_local):
    peers = lax.axis_size("orb")
    parts = lax.axis_size("fft")
    orb_dev, rows_x, width = orbitals.shape
    fits = rows_x == 8 * peers and width == LANES * parts and peers % 4 == 0
    fits = fits and orb_dev == 8 and partner_local.shape[0] == 8 and orb_dev * peers <= LANES
    step = fused_device if fits else plain_device
    return step(orbitals, kernel, partner_owner, partner_local)


def solution(mesh):
    in_specs = (P("orb", "fft", None), P("fft", None), P("orb", None, None), P("orb", None))
    out_specs = P("orb", "fft", None)
    return jax.shard_map(
        on_device, mesh=mesh, in_specs=in_specs, out_specs=out_specs, check_vma=False
    )
```

```python
import functools
import math

import jax
import jax.numpy as jnp
import numpy as np
from jax import lax
from jax.experimental import pallas as pl
from jax.experimental.pallas import tpu as pltpu
from jax.sharding import PartitionSpec as P

LEVELS = 32767.0
STEPS = 128.0
LANES = 128


def angles(length):
    series = np.arange(length)
    return (series[:, None] * series[None, :] % length) * (2.0 * math.pi / length)


def packed_tables(length):
    half = length // 2
    angle = angles(length)[:, :half]
    sine = np.sin(angle)
    sine[:, 0] = np.cos(math.pi * np.arange(length))
    forward = np.concatenate([np.cos(angle), sine], axis=1)
    gain = np.full((2 * half,), 2.0)
    gain[0] = gain[half] = 1.0
    backward = (forward * gain).T
    return forward.astype(np.float32), backward.astype(np.float32)


def product(form, left, right):
    return jnp.einsum(form, left, right, precision=lax.Precision.HIGH, preferred_element_type=jnp.float32)


def weights(kernel):
    half = kernel.shape[0] // 2
    mirror = jnp.roll(jnp.flip(kernel, (0, 1)), 1, (0, 1))
    even = (0.5 * (kernel + mirror)).T
    plus = even[:, :half]
    minus = jnp.concatenate([even[:, half : half + 1], even[:, 1:half]], axis=1)
    return plus, minus


def convolve(density, kernel):
    full_x, width_y = density.shape[1:]
    half = width_y // 2
    forward, backward = packed_tables(width_y)
    angle = angles(full_x)
    both = np.concatenate([np.cos(angle), np.sin(angle)], axis=0).astype(np.float32)
    plus, minus = weights(kernel)
    scale = 1.0 / (full_x * width_y)
    weight = jnp.concatenate([plus, minus], axis=1) * scale
    spread = product("txy,yk->txk", density, forward)
    mixed = product("qx,txk->tqk", both, spread)
    cos_part = mixed[:, :full_x] * weight
    sin_part = mixed[:, full_x:] * weight
    first = cos_part[:, :, :half] - sin_part[:, :, half:]
    second = sin_part[:, :, :half] + cos_part[:, :, half:]
    back = product("qx,txk->tqk", both, jnp.concatenate([first, second], axis=2))
    cos_part = back[:, :full_x]
    sin_part = back[:, full_x:]
    real = cos_part[:, :, :half] + sin_part[:, :, half:]
    imag = cos_part[:, :, half:] - sin_part[:, :, :half]
    return product("txk,ky->txy", jnp.concatenate([real, imag], axis=2), backward)


def encode(values, run):
    rows, width = values.shape
    runs = values.reshape(rows, width // run, run)
    peak = jnp.maximum(jnp.max(jnp.abs(runs), axis=2), 1e-30)
    level = jnp.ceil(jnp.log2(peak) * STEPS + 0.01)
    rate = jnp.exp2(level / STEPS)
    coded = jnp.round(runs * (LEVELS / rate)[:, :, None]).reshape(rows, width)
    extra = jnp.pad(level, ((0, 0), (0, LANES - width // run)))
    return jnp.concatenate([coded, extra], axis=1).astype(jnp.int16)


def decode(coded, run):
    rows = coded.shape[0]
    width = coded.shape[1] - LANES
    level = coded[:, width : width + width // run].astype(jnp.float32)
    rate = jnp.exp2(level / STEPS) / LEVELS
    runs = coded[:, :width].astype(jnp.float32).reshape(rows, width // run, run)
    return (runs * rate[:, :, None]).reshape(rows, width)


def plain_device(orbitals, kernel, partner_owner, partner_local):
    peers = lax.axis_size("orb")
    parts = lax.axis_size("fft")
    orb_dev, rows_x, width_y = orbitals.shape
    tasks_dev = partner_local.shape[0]
    tasks = tasks_dev * peers
    norb = orb_dev * peers
    full_x = rows_x * parts
    chunk = rows_x * width_y // peers
    run = min(width_y, chunk)
    own = tasks // (peers * parts)

    whole = lax.all_to_all(
        jnp.broadcast_to(kernel[None], (parts,) + kernel.shape), "fft", 0, 0, tiled=True
    ).reshape(parts * kernel.shape[0], kernel.shape[1])
    named = partner_owner[:, :, 0] * orb_dev + partner_local
    named = jnp.broadcast_to(named[None], (peers, tasks_dev, 2))
    pair_ids = lax.all_to_all(named, "orb", 0, 0, tiled=True).reshape(tasks, 2)
    held = lax.all_to_all(
        orbitals.reshape(orb_dev, peers, chunk).transpose(1, 0, 2), "orb", 0, 0, tiled=True
    ).reshape(norb, chunk)

    pick = (pair_ids.T.reshape(2 * tasks, 1) == jnp.arange(norb, dtype=jnp.int32)[None, :]).astype(jnp.bfloat16)
    chosen = jnp.dot(pick, held, preferred_element_type=jnp.float32)
    first, second = chosen[:tasks], chosen[tasks:]
    density = first * second

    sent = encode(density, run).reshape(parts, peers, own, chunk + LANES)
    got = lax.all_to_all(sent.reshape(parts * peers * own, chunk + LANES), ("fft", "orb"), 0, 0, tiled=True)
    grid = decode(got, run).reshape(parts * peers, own, chunk)
    grid = grid.transpose(1, 0, 2).reshape(own, full_x, width_y)
    potential = convolve(grid, whole)
    potential = potential.reshape(own, parts * peers, chunk).transpose(1, 0, 2)
    sent = encode(potential.reshape(parts * peers * own, chunk), run)
    got = lax.all_to_all(sent, ("fft", "orb"), 0, 0, tiled=True)
    potential = decode(got, run)

    terms = jnp.concatenate([potential * second, potential * first], axis=0)
    high = lax.reduce_precision(terms, 8, 7)
    low = (terms - high).astype(jnp.bfloat16)
    high = high.astype(jnp.bfloat16)
    total = jnp.einsum(
        "to,tc->oc",
        jnp.concatenate([pick, pick], axis=0),
        jnp.concatenate([high, low], axis=0),
        preferred_element_type=jnp.float32,
    )
    sent = encode(-total, run)
    got = decode(lax.all_to_all(sent, "orb", 0, 0, tiled=True), run)
    return got.reshape(peers, orb_dev, chunk).transpose(1, 0, 2).reshape(orb_dev, rows_x, width_y)


F32 = jnp.float32
BF16 = jnp.bfloat16
MESH = pl.DeviceIdType.MESH


def split(values):
    high = values.astype(BF16)
    return high, (values - high.astype(F32)).astype(BF16)


def dot(left, right):
    return jnp.dot(left, right, preferred_element_type=F32)


def left_table(table, values):
    high, low = split(values)
    return dot(table[0], high) + dot(table[0], low) + dot(table[1], high)


def right_table(values, table):
    high, low = split(values)
    return dot(high, table[0]) + dot(low, table[0]) + dot(high, table[1])


def iota(shape, axis):
    return lax.broadcasted_iota(jnp.int32, shape, axis)


def quantize(values, first_row=0):
    count, rows, _ = values.shape
    peak = jnp.maximum(jnp.max(jnp.abs(values), axis=2, keepdims=True), 1e-30)
    coded = jnp.round(values * (LEVELS / peak)).astype(jnp.int32).astype(jnp.int16)
    shape = (count, rows, LANES)
    spot = iota(shape, 2) == iota(shape, 1) + first_row
    scale = jnp.sum(jnp.where(spot, peak * (1.0 / LEVELS), 0.0), axis=1, keepdims=True)
    return coded, scale


def restore(coded, scale, first_row=0):
    count, rows, _ = coded.shape
    shape = (count, rows, LANES)
    spot = iota(shape, 2) == iota(shape, 1) + first_row
    rate = jnp.sum(jnp.where(spot, jnp.broadcast_to(scale, shape), 0.0), axis=2, keepdims=True)
    return coded.astype(jnp.int32).astype(F32) * rate


def half_roll(values):
    parts = [
        pltpu.roll(values[:, at : at + LANES], LANES // 2, 1) for at in range(0, values.shape[1], LANES)
    ]
    return jnp.concatenate(parts, axis=1)


def fused(
    peers, parts, rows, orb_dev, task_dev,
    orb_ref, ids_ref, ker_ref, fwd_ref, bwd_ref, both_ref, coded_ref, rate_ref,
    held, names, whole, chosen, snd1, rec1, sc_snd1, sc_rec1, snd2, rec2, sc_snd2, sc_rec2,
    hots, turned_hots, acc, snd3, rec3, sc_snd3, sc_rec3, send_sem, recv_sem,
):
    o = lax.axis_index("orb")
    f = lax.axis_index("fft")
    everyone = peers * parts
    me = f * peers + o
    tasks = task_dev * peers
    width = orb_ref.shape[2]
    half = width // 2
    full_x = ker_ref.shape[2]
    deep = snd1.shape[2]
    chunks = snd1.shape[0]
    step = peers * deep
    total_rows = tasks * rows
    norb_rows = peers * orb_dev * rows
    pack = deep // rows

    barrier = pltpu.get_barrier_semaphore()

    def greet(i, c):
        p = lax.rem(me + i, everyone)
        pl.semaphore_signal(barrier, inc=1, device_id=(lax.rem(p, peers), p // peers), device_id_type=MESH)
        return c

    lax.fori_loop(1, everyone, greet, 0)
    pl.semaphore_wait(barrier, everyone - 1)

    def remote(src, dst, k, device):
        return pltpu.make_async_remote_copy(
            src_ref=src, dst_ref=dst, send_sem=send_sem.at[k], recv_sem=recv_sem.at[k],
            device_id=device, device_id_type=MESH,
        )

    def over_orb(src, dst, k, fixed=False):
        def one(i, c):
            p = lax.rem(o + i, peers)
            remote(src if fixed else src.at[p], dst.at[o], k, (p, f)).start()
            return c

        pltpu.make_async_copy(src if fixed else src.at[o], dst.at[o], recv_sem.at[k]).start()
        lax.fori_loop(1, peers, one, 0)

    def over_all(i, scale, scale_to, src, dst, k):
        def one(j, c):
            p = lax.rem(me + j, everyone)
            device = (lax.rem(p, peers), p // peers)
            remote(scale.at[i, p], scale_to.at[i, me], k + i, device).start()
            remote(src.at[i, p], dst.at[i, me], k + chunks + i, device).start()
            return c

        pltpu.make_async_copy(scale.at[i, me], scale_to.at[i, me], recv_sem.at[k + i]).start()
        pltpu.make_async_copy(src.at[i, me], dst.at[i, me], recv_sem.at[k + chunks + i]).start()
        lax.fori_loop(1, everyone, one, 0)

    def arrived(dst, k):
        pltpu.make_async_copy(dst, dst, recv_sem.at[k]).wait()

    def left(dst, k):
        gone = dst.at[pl.ds(0, dst.shape[0] - 1)]
        pltpu.make_async_copy(gone, gone, send_sem.at[k]).wait()

    over_orb(ids_ref, names, 0, fixed=True)
    over_orb(orb_ref, held, 1)

    def halves(i, c):
        p = lax.rem(f + i, parts)
        remote(ker_ref.at[0], whole.at[f], 2, (o, p)).start()
        return c

    pltpu.make_async_copy(ker_ref.at[0], whole.at[f], recv_sem.at[2]).start()
    lax.fori_loop(1, parts, halves, 0)

    def task_of(row):
        return row // deep % peers * task_dev + row // step * pack + row // rows % pack

    arrived(names, 0)
    named = names[...].reshape(tasks, LANES)
    grow = (task_of(iota((total_rows, tasks), 0)) == iota((total_rows, tasks), 1)).astype(F32).astype(BF16)
    down = dot(grow, named.astype(BF16)).astype(jnp.int32) * rows + iota((total_rows, LANES), 0) % rows
    spread = (task_of(iota((tasks, total_rows), 1)) == iota((tasks, total_rows), 0)).astype(F32).astype(BF16)
    across = dot(named.T[:8].astype(BF16), spread).astype(jnp.int32) * rows + iota((8, total_rows), 1) % rows
    for i in range(chunks):
        at = slice(i * step, (i + 1) * step)
        for c in range(2):
            hot = down[at, c : c + 1] == iota((step, norb_rows), 1)
            hots[c, at, :] = hot.astype(F32).astype(BF16)
            hot = across[c : c + 1, at] == iota((norb_rows, step), 0)
            turned_hots[i, :, c * step : (c + 1) * step] = hot.astype(F32).astype(BF16)

    arrived(whole, 2)
    per = half // parts
    turned = split(whole[...].reshape(width, full_x).T)
    lane = iota((width, LANES), 1)
    freq = f * per + lax.rem(lane, per)
    freq = jnp.where((lane >= per) & (freq == 0), half, freq)
    row = iota((width, LANES), 0)
    straight = (row == freq).astype(F32).astype(BF16)
    mirror = (row == lax.rem(width - freq, width)).astype(F32).astype(BF16)
    flip_shape = (full_x, full_x)
    flip = (iota(flip_shape, 1) == lax.rem(full_x - iota(flip_shape, 0), full_x)).astype(F32).astype(BF16)
    plain = dot(turned[0], straight) + dot(turned[1], straight)
    other = split(dot(turned[0], mirror) + dot(turned[1], mirror))
    weight = (plain + dot(flip, other[0]) + dot(flip, other[1])) * (0.5 / (full_x * width))
    sign = jnp.where(iota((full_x, pack * LANES), 1) % LANES < per, 1.0, -1.0)
    weight = jnp.concatenate([weight] * pack, axis=1)
    signed = weight * sign

    arrived(held, 1)
    source = held[...].reshape(norb_rows, width)
    for i in range(chunks):
        at = slice(i * step, (i + 1) * step)
        pair = []
        for c in range(2):
            value = dot(hots[c, at, :], source)
            chosen[c, at, :] = value.astype(BF16)
            pair.append(value)
        waves = right_table(pair[0] * pair[1], fwd_ref)
        for h in range(parts):
            coded, scale = quantize(waves[:, h * LANES : (h + 1) * LANES].reshape(peers, deep, LANES))
            snd1[i, h * peers : (h + 1) * peers] = coded
            sc_snd1[i, h * peers : (h + 1) * peers] = scale
        over_all(i, sc_snd1, sc_rec1, snd1, rec1, 3)

    for i in range(chunks):
        arrived(sc_rec1.at[i], 3 + i)
        arrived(rec1.at[i], 3 + chunks + i)
        values = restore(rec1[i], sc_rec1[i])
        grid = jnp.concatenate(
            [values[:, t * rows : (t + 1) * rows].reshape(full_x, LANES) for t in range(pack)], axis=1
        )
        mixed = left_table(both_ref, grid)
        mixed = mixed[:full_x] * weight + half_roll(mixed[full_x:] * signed)
        mixed = left_table(both_ref, mixed)
        mixed = mixed[:full_x] + half_roll(mixed[full_x:]) * sign
        values = jnp.concatenate(
            [mixed[:, t * LANES : (t + 1) * LANES].reshape(everyone, rows, LANES) for t in range(pack)], axis=1
        )
        coded, scale = quantize(values)
        snd2[i] = coded
        sc_snd2[i] = scale
        over_all(i, sc_snd2, sc_rec2, snd2, rec2, 3 + 2 * chunks)

    last = 3 + 4 * chunks
    for i in range(chunks):
        at = slice(i * step, (i + 1) * step)
        arrived(sc_rec2.at[i], 3 + 2 * chunks + i)
        arrived(rec2.at[i], 3 + 3 * chunks + i)
        waves = []
        for h in range(parts):
            spot = slice(h * peers, (h + 1) * peers)
            waves.append(restore(rec2[i, spot], sc_rec2[i, spot]).reshape(step, LANES))
        potential = right_table(jnp.concatenate(waves, axis=1), bwd_ref)
        high, low = split(
            jnp.concatenate([potential * chosen[1 - c, at, :].astype(F32) for c in range(2)], axis=0)
        )
        if i < chunks - 1:
            term = dot(turned_hots[i], high) + dot(turned_hots[i], low)
            acc[...] = term if i == 0 else acc[...] + term
            continue
        some = norb_rows // 4
        group = peers // 4
        for n in range(4):
            b = lax.rem(o // group + n + 1, 4)
            here = pl.ds(pl.multiple_of(b * some, some), some)
            hot = turned_hots[i, here, :]
            total = -(acc[here, :] + dot(hot, high) + dot(hot, low))
            coded, scale = quantize(total.reshape(group, orb_dev * rows, width))
            snd3[pl.ds(b * group, group)] = coded
            sc_snd3[pl.ds(b * group, group)] = scale

            def deliver(j, c):
                p = b * group + j

                @pl.when(p != o)
                def _():
                    remote(sc_snd3.at[p], sc_rec3.at[o], last, (p, f)).start()
                    remote(snd3.at[p], rec3.at[o], last + 1, (p, f)).start()

                @pl.when(p == o)
                def _():
                    pltpu.make_async_copy(sc_snd3.at[p], sc_rec3.at[o], recv_sem.at[last]).start()
                    pltpu.make_async_copy(snd3.at[p], rec3.at[o], recv_sem.at[last + 1]).start()

                return c

            lax.fori_loop(0, group, deliver, 0)

    left(names, 0)
    left(held, 1)
    gone = whole.at[pl.ds(0, parts - 1)]
    pltpu.make_async_copy(gone, gone, send_sem.at[2]).wait()
    for i in range(chunks):
        left(sc_snd1.at[i], 3 + i)
        left(snd1.at[i], 3 + chunks + i)
        left(sc_snd2.at[i], 3 + 2 * chunks + i)
        left(snd2.at[i], 3 + 3 * chunks + i)
    arrived(sc_rec3, last)
    arrived(rec3, last + 1)
    coded_ref[...] = rec3[...]
    rate_ref[...] = sc_rec3[...]
    left(sc_snd3, last)
    left(snd3, last + 1)


def unpack(rows, coded_ref, rate_ref, out_ref):
    count, block, width = coded_ref.shape
    for p in range(count):
        values = restore(coded_ref[p : p + 1], rate_ref[p : p + 1])
        out_ref[:, p * rows : (p + 1) * rows, :] = values.reshape(block // rows, rows, width)


def tables_of(array):
    exact = jnp.asarray(array, F32)
    high = lax.reduce_precision(exact, 8, 7)
    return jnp.stack([high.astype(BF16), (exact - high).astype(BF16)])


def fused_device(orbitals, kernel, partner_owner, partner_local):
    peers = lax.axis_size("orb")
    parts = lax.axis_size("fft")
    orb_dev, rows_x, width = orbitals.shape
    task_dev = partner_local.shape[0]
    rows = rows_x // peers
    full_x = rows_x * parts
    everyone = peers * parts
    block = orb_dev * rows
    half = width // 2
    per = half // parts

    named = (partner_owner[:, :, 0] * orb_dev + partner_local).astype(F32)
    named = jnp.pad(named, ((0, 0), (0, LANES - 2)))
    sent = orbitals.reshape(orb_dev, peers, rows, width).transpose(1, 0, 2, 3).reshape(peers, block, width)
    forward, backward = packed_tables(width)
    order = np.concatenate(
        [np.concatenate([np.arange(h * per, (h + 1) * per), half + np.arange(h * per, (h + 1) * per)]) for h in range(parts)]
    )
    angle = angles(full_x)
    both = np.concatenate([np.cos(angle), np.sin(angle)], axis=0)
    vmem = pl.BlockSpec(memory_space=pltpu.VMEM)
    pack = 2
    chunks = task_dev // pack
    deep = pack * rows
    ways = [
        pltpu.VMEM((chunks, everyone, deep, LANES), jnp.int16), pltpu.VMEM((chunks, everyone, deep, LANES), jnp.int16),
        pltpu.VMEM((chunks, everyone, 1, LANES), F32), pltpu.VMEM((chunks, everyone, 1, LANES), F32),
    ]
    rows_all = task_dev * peers * rows
    orb_rows = peers * block
    sems = 5 + 4 * chunks
    coded, rate = pl.pallas_call(
        functools.partial(fused, peers, parts, rows, orb_dev, task_dev),
        out_shape=(
            jax.ShapeDtypeStruct((peers, block, width), jnp.int16),
            jax.ShapeDtypeStruct((peers, 1, LANES), F32),
        ),
        in_specs=[vmem] * 6,
        out_specs=(vmem, vmem),
        scratch_shapes=[
            pltpu.VMEM((peers, block, width), BF16),
            pltpu.VMEM((peers, task_dev, LANES), F32),
            pltpu.VMEM((parts,) + kernel.shape, F32),
            pltpu.VMEM((2, rows_all, width), BF16),
            *ways, *ways,
            pltpu.VMEM((2, rows_all, orb_rows), BF16),
            pltpu.VMEM((chunks, orb_rows, 2 * rows_all // chunks), BF16),
            pltpu.VMEM((orb_rows, width), F32),
            pltpu.VMEM((peers, block, width), jnp.int16), pltpu.VMEM((peers, block, width), jnp.int16),
            pltpu.VMEM((peers, 1, LANES), F32), pltpu.VMEM((peers, 1, LANES), F32),
            pltpu.SemaphoreType.DMA((sems,)),
            pltpu.SemaphoreType.DMA((sems,)),
        ],
        compiler_params=pltpu.CompilerParams(
            collective_id=0, has_side_effects=True, vmem_limit_bytes=48 * 1024 * 1024
        ),
    )(sent, named, kernel[None], tables_of(forward[:, order]), tables_of(backward[order]), tables_of(both))
    group = peers // 4
    return pl.pallas_call(
        functools.partial(unpack, rows),
        grid=(4,),
        out_shape=jax.ShapeDtypeStruct((orb_dev, rows_x, width), F32),
        in_specs=[
            pl.BlockSpec((group, block, width), lambda i: (i, 0, 0)),
            pl.BlockSpec((group, 1, LANES), lambda i: (i, 0, 0)),
        ],
        out_specs=pl.BlockSpec((orb_dev, group * rows, width), lambda i: (0, i, 0)),
    )(coded, rate)


def on_device(orbitals, kernel, partner_owner, partner_local):
    peers = lax.axis_size("orb")
    parts = lax.axis_size("fft")
    orb_dev, rows_x, width = orbitals.shape
    fits = rows_x == 8 * peers and width == LANES * parts and peers % 4 == 0
    fits = fits and orb_dev == 8 and partner_local.shape[0] == 8 and orb_dev * peers <= LANES
    step = fused_device if fits else plain_device
    return step(orbitals, kernel, partner_owner, partner_local)


def solution(mesh):
    in_specs = (P("orb", "fft", None), P("fft", None), P("orb", None, None), P("orb", None))
    out_specs = P("orb", "fft", None)
    return jax.shard_map(
        on_device, mesh=mesh, in_specs=in_specs, out_specs=out_specs, check_vma=False
    )
```

```python
import functools
import math

import jax
import jax.numpy as jnp
import numpy as np
from jax import lax
from jax.experimental import pallas as pl
from jax.experimental.pallas import tpu as pltpu
from jax.sharding import PartitionSpec as P

LEVELS = 32767.0
STEPS = 128.0
LANES = 128


def angles(length):
    series = np.arange(length)
    return (series[:, None] * series[None, :] % length) * (2.0 * math.pi / length)


def packed_tables(length):
    half = length // 2
    angle = angles(length)[:, :half]
    sine = np.sin(angle)
    sine[:, 0] = np.cos(math.pi * np.arange(length))
    forward = np.concatenate([np.cos(angle), sine], axis=1)
    gain = np.full((2 * half,), 2.0)
    gain[0] = gain[half] = 1.0
    backward = (forward * gain).T
    return forward.astype(np.float32), backward.astype(np.float32)


def product(form, left, right):
    return jnp.einsum(form, left, right, precision=lax.Precision.HIGH, preferred_element_type=jnp.float32)


def weights(kernel):
    half = kernel.shape[0] // 2
    mirror = jnp.roll(jnp.flip(kernel, (0, 1)), 1, (0, 1))
    even = (0.5 * (kernel + mirror)).T
    plus = even[:, :half]
    minus = jnp.concatenate([even[:, half : half + 1], even[:, 1:half]], axis=1)
    return plus, minus


def convolve(density, kernel):
    full_x, width_y = density.shape[1:]
    half = width_y // 2
    forward, backward = packed_tables(width_y)
    angle = angles(full_x)
    both = np.concatenate([np.cos(angle), np.sin(angle)], axis=0).astype(np.float32)
    plus, minus = weights(kernel)
    scale = 1.0 / (full_x * width_y)
    weight = jnp.concatenate([plus, minus], axis=1) * scale
    spread = product("txy,yk->txk", density, forward)
    mixed = product("qx,txk->tqk", both, spread)
    cos_part = mixed[:, :full_x] * weight
    sin_part = mixed[:, full_x:] * weight
    first = cos_part[:, :, :half] - sin_part[:, :, half:]
    second = sin_part[:, :, :half] + cos_part[:, :, half:]
    back = product("qx,txk->tqk", both, jnp.concatenate([first, second], axis=2))
    cos_part = back[:, :full_x]
    sin_part = back[:, full_x:]
    real = cos_part[:, :, :half] + sin_part[:, :, half:]
    imag = cos_part[:, :, half:] - sin_part[:, :, :half]
    return product("txk,ky->txy", jnp.concatenate([real, imag], axis=2), backward)


def encode(values, run):
    rows, width = values.shape
    runs = values.reshape(rows, width // run, run)
    peak = jnp.maximum(jnp.max(jnp.abs(runs), axis=2), 1e-30)
    level = jnp.ceil(jnp.log2(peak) * STEPS + 0.01)
    rate = jnp.exp2(level / STEPS)
    coded = jnp.round(runs * (LEVELS / rate)[:, :, None]).reshape(rows, width)
    extra = jnp.pad(level, ((0, 0), (0, LANES - width // run)))
    return jnp.concatenate([coded, extra], axis=1).astype(jnp.int16)


def decode(coded, run):
    rows = coded.shape[0]
    width = coded.shape[1] - LANES
    level = coded[:, width : width + width // run].astype(jnp.float32)
    rate = jnp.exp2(level / STEPS) / LEVELS
    runs = coded[:, :width].astype(jnp.float32).reshape(rows, width // run, run)
    return (runs * rate[:, :, None]).reshape(rows, width)


def plain_device(orbitals, kernel, partner_owner, partner_local):
    peers = lax.axis_size("orb")
    parts = lax.axis_size("fft")
    orb_dev, rows_x, width_y = orbitals.shape
    tasks_dev = partner_local.shape[0]
    tasks = tasks_dev * peers
    norb = orb_dev * peers
    full_x = rows_x * parts
    chunk = rows_x * width_y // peers
    run = min(width_y, chunk)
    own = tasks // (peers * parts)

    whole = lax.all_to_all(
        jnp.broadcast_to(kernel[None], (parts,) + kernel.shape), "fft", 0, 0, tiled=True
    ).reshape(parts * kernel.shape[0], kernel.shape[1])
    named = partner_owner[:, :, 0] * orb_dev + partner_local
    named = jnp.broadcast_to(named[None], (peers, tasks_dev, 2))
    pair_ids = lax.all_to_all(named, "orb", 0, 0, tiled=True).reshape(tasks, 2)
    held = lax.all_to_all(
        orbitals.reshape(orb_dev, peers, chunk).transpose(1, 0, 2), "orb", 0, 0, tiled=True
    ).reshape(norb, chunk)

    pick = (pair_ids.T.reshape(2 * tasks, 1) == jnp.arange(norb, dtype=jnp.int32)[None, :]).astype(jnp.bfloat16)
    chosen = jnp.dot(pick, held, preferred_element_type=jnp.float32)
    first, second = chosen[:tasks], chosen[tasks:]
    density = first * second

    sent = encode(density, run).reshape(parts, peers, own, chunk + LANES)
    got = lax.all_to_all(sent.reshape(parts * peers * own, chunk + LANES), ("fft", "orb"), 0, 0, tiled=True)
    grid = decode(got, run).reshape(parts * peers, own, chunk)
    grid = grid.transpose(1, 0, 2).reshape(own, full_x, width_y)
    potential = convolve(grid, whole)
    potential = potential.reshape(own, parts * peers, chunk).transpose(1, 0, 2)
    sent = encode(potential.reshape(parts * peers * own, chunk), run)
    got = lax.all_to_all(sent, ("fft", "orb"), 0, 0, tiled=True)
    potential = decode(got, run)

    terms = jnp.concatenate([potential * second, potential * first], axis=0)
    high = lax.reduce_precision(terms, 8, 7)
    low = (terms - high).astype(jnp.bfloat16)
    high = high.astype(jnp.bfloat16)
    total = jnp.einsum(
        "to,tc->oc",
        jnp.concatenate([pick, pick], axis=0),
        jnp.concatenate([high, low], axis=0),
        preferred_element_type=jnp.float32,
    )
    sent = encode(-total, run)
    got = decode(lax.all_to_all(sent, "orb", 0, 0, tiled=True), run)
    return got.reshape(peers, orb_dev, chunk).transpose(1, 0, 2).reshape(orb_dev, rows_x, width_y)


F32 = jnp.float32
BF16 = jnp.bfloat16
MESH = pl.DeviceIdType.MESH


def split(values):
    high = values.astype(BF16)
    return high, (values - high.astype(F32)).astype(BF16)


def dot(left, right):
    return jnp.dot(left, right, preferred_element_type=F32)


def left_table(table, values):
    high, low = split(values)
    return dot(table[0], high) + dot(table[0], low) + dot(table[1], high)


def right_table(values, table):
    high, low = split(values)
    return dot(high, table[0]) + dot(low, table[0]) + dot(high, table[1])


def iota(shape, axis):
    return lax.broadcasted_iota(jnp.int32, shape, axis)


def quantize(values, first_row=0):
    count, rows, _ = values.shape
    peak = jnp.maximum(jnp.max(jnp.abs(values), axis=2, keepdims=True), 1e-30)
    coded = jnp.round(values * (LEVELS / peak)).astype(jnp.int32).astype(jnp.int16)
    shape = (count, rows, LANES)
    spot = iota(shape, 2) == iota(shape, 1) + first_row
    scale = jnp.sum(jnp.where(spot, peak * (1.0 / LEVELS), 0.0), axis=1, keepdims=True)
    return coded, scale


def restore(coded, scale, first_row=0):
    count, rows, _ = coded.shape
    shape = (count, rows, LANES)
    spot = iota(shape, 2) == iota(shape, 1) + first_row
    rate = jnp.sum(jnp.where(spot, jnp.broadcast_to(scale, shape), 0.0), axis=2, keepdims=True)
    return coded.astype(jnp.int32).astype(F32) * rate


def half_roll(values):
    parts = [
        pltpu.roll(values[:, at : at + LANES], LANES // 2, 1) for at in range(0, values.shape[1], LANES)
    ]
    return jnp.concatenate(parts, axis=1)


def fused(
    peers, parts, rows, orb_dev, task_dev,
    orb_ref, owner_ref, local_ref, ker_ref, fwd_hbm, bwd_hbm, both_hbm, coded_ref, rate_ref,
    ids, fwd_ref, bwd_ref, both_ref, held, names, whole, chosen, snd1, rec1, sc_snd1, sc_rec1, snd2, rec2, sc_snd2, sc_rec2,
    hots, turned_hots, acc, snd3, rec3, sc_snd3, sc_rec3, send_sem, recv_sem, table_sem,
):
    o = lax.axis_index("orb")
    f = lax.axis_index("fft")
    everyone = peers * parts
    me = f * peers + o
    tasks = task_dev * peers
    width = orb_ref.shape[2]
    half = width // 2
    full_x = ker_ref.shape[1]
    deep = snd1.shape[2]
    chunks = snd1.shape[0]
    step = peers * deep
    total_rows = tasks * rows
    norb_rows = peers * orb_dev * rows
    pack = deep // rows

    fetches = [
        pltpu.make_async_copy(src, dst, table_sem.at[n])
        for n, (src, dst) in enumerate(((fwd_hbm, fwd_ref), (bwd_hbm, bwd_ref), (both_hbm, both_ref)))
    ]
    for fetch in fetches:
        fetch.start()
    table = jnp.zeros((task_dev, LANES), F32)
    for t in range(task_dev):
        for c in range(2):
            spot = (iota(table.shape, 0) == t) & (iota(table.shape, 1) == c)
            table = jnp.where(spot, (owner_ref[c, 0, t] * orb_dev + local_ref[c, t]).astype(F32), table)
    ids[...] = table

    barrier = pltpu.get_barrier_semaphore()

    def greet(i, c):
        p = lax.rem(me + i, everyone)
        pl.semaphore_signal(barrier, inc=1, device_id=(lax.rem(p, peers), p // peers), device_id_type=MESH)
        return c

    lax.fori_loop(1, everyone, greet, 0)
    pl.semaphore_wait(barrier, everyone - 1)

    def remote(src, dst, k, device):
        return pltpu.make_async_remote_copy(
            src_ref=src, dst_ref=dst, send_sem=send_sem.at[k], recv_sem=recv_sem.at[k],
            device_id=device, device_id_type=MESH,
        )

    def over_orb(piece, dst, k):
        def one(i, c):
            p = lax.rem(o + i, peers)
            remote(piece(p), dst.at[o], k, (p, f)).start()
            return c

        pltpu.make_async_copy(piece(o), dst.at[o], recv_sem.at[k]).start()
        lax.fori_loop(1, peers, one, 0)

    def over_all(i, scale, scale_to, src, dst, k):
        def one(j, c):
            p = lax.rem(me + j, everyone)
            device = (lax.rem(p, peers), p // peers)
            remote(scale.at[i, p], scale_to.at[i, me], k + i, device).start()
            remote(src.at[i, p], dst.at[i, me], k + chunks + i, device).start()
            return c

        pltpu.make_async_copy(scale.at[i, me], scale_to.at[i, me], recv_sem.at[k + i]).start()
        pltpu.make_async_copy(src.at[i, me], dst.at[i, me], recv_sem.at[k + chunks + i]).start()
        lax.fori_loop(1, everyone, one, 0)

    def arrived(dst, k):
        pltpu.make_async_copy(dst, dst, recv_sem.at[k]).wait()

    def left(dst, k):
        gone = dst.at[pl.ds(0, dst.shape[0] - 1)]
        pltpu.make_async_copy(gone, gone, send_sem.at[k]).wait()

    over_orb(lambda p: ids, names, 0)
    over_orb(lambda p: orb_ref.at[:, pl.ds(pl.multiple_of(p * rows, rows), rows), :], held, 1)

    def halves(i, c):
        p = lax.rem(f + i, parts)
        remote(ker_ref, whole.at[f], 2, (o, p)).start()
        return c

    pltpu.make_async_copy(ker_ref, whole.at[f], recv_sem.at[2]).start()
    lax.fori_loop(1, parts, halves, 0)

    def task_of(row):
        return row // deep % peers * task_dev + row // step * pack + row // rows % pack

    arrived(names, 0)
    named = names[...].reshape(tasks, LANES)
    grow = (task_of(iota((total_rows, tasks), 0)) == iota((total_rows, tasks), 1)).astype(F32).astype(BF16)
    down = dot(grow, named.astype(BF16)).astype(jnp.int32) * rows + iota((total_rows, LANES), 0) % rows
    spread = (task_of(iota((tasks, total_rows), 1)) == iota((tasks, total_rows), 0)).astype(F32).astype(BF16)
    across = dot(named.T[:8].astype(BF16), spread).astype(jnp.int32) * rows + iota((8, total_rows), 1) % rows
    for i in range(chunks):
        at = slice(i * step, (i + 1) * step)
        for c in range(2):
            hot = down[at, c : c + 1] == iota((step, norb_rows), 1)
            hots[c, at, :] = hot.astype(F32).astype(BF16)
            hot = across[c : c + 1, at] == iota((norb_rows, step), 0)
            turned_hots[i, :, c * step : (c + 1) * step] = hot.astype(F32).astype(BF16)

    arrived(whole, 2)
    per = half // parts
    turned = split(whole[...].reshape(width, full_x).T)
    lane = iota((width, LANES), 1)
    freq = f * per + lax.rem(lane, per)
    freq = jnp.where((lane >= per) & (freq == 0), half, freq)
    row = iota((width, LANES), 0)
    straight = (row == freq).astype(F32).astype(BF16)
    mirror = (row == lax.rem(width - freq, width)).astype(F32).astype(BF16)
    flip_shape = (full_x, full_x)
    flip = (iota(flip_shape, 1) == lax.rem(full_x - iota(flip_shape, 0), full_x)).astype(F32).astype(BF16)
    plain = dot(turned[0], straight) + dot(turned[1], straight)
    other = split(dot(turned[0], mirror) + dot(turned[1], mirror))
    weight = (plain + dot(flip, other[0]) + dot(flip, other[1])) * (0.5 / (full_x * width))
    sign = jnp.where(iota((full_x, pack * LANES), 1) % LANES < per, 1.0, -1.0)
    weight = jnp.concatenate([weight] * pack, axis=1)
    signed = weight * sign

    for fetch in fetches:
        fetch.wait()
    arrived(held, 1)
    source = held[...].reshape(norb_rows, width)
    for i in range(chunks):
        at = slice(i * step, (i + 1) * step)
        pair = []
        for c in range(2):
            value = dot(hots[c, at, :], source)
            chosen[c, at, :] = value.astype(BF16)
            pair.append(value)
        waves = right_table(pair[0] * pair[1], fwd_ref)
        for h in range(parts):
            coded, scale = quantize(waves[:, h * LANES : (h + 1) * LANES].reshape(peers, deep, LANES))
            snd1[i, h * peers : (h + 1) * peers] = coded
            sc_snd1[i, h * peers : (h + 1) * peers] = scale
        over_all(i, sc_snd1, sc_rec1, snd1, rec1, 3)

    for i in range(chunks):
        arrived(sc_rec1.at[i], 3 + i)
        arrived(rec1.at[i], 3 + chunks + i)
        values = restore(rec1[i], sc_rec1[i])
        grid = jnp.concatenate(
            [values[:, t * rows : (t + 1) * rows].reshape(full_x, LANES) for t in range(pack)], axis=1
        )
        mixed = left_table(both_ref, grid)
        mixed = mixed[:full_x] * weight + half_roll(mixed[full_x:] * signed)
        mixed = left_table(both_ref, mixed)
        mixed = mixed[:full_x] + half_roll(mixed[full_x:]) * sign
        values = jnp.concatenate(
            [mixed[:, t * LANES : (t + 1) * LANES].reshape(everyone, rows, LANES) for t in range(pack)], axis=1
        )
        coded, scale = quantize(values)
        snd2[i] = coded
        sc_snd2[i] = scale
        over_all(i, sc_snd2, sc_rec2, snd2, rec2, 3 + 2 * chunks)

    last = 3 + 4 * chunks
    for i in range(chunks):
        at = slice(i * step, (i + 1) * step)
        arrived(sc_rec2.at[i], 3 + 2 * chunks + i)
        arrived(rec2.at[i], 3 + 3 * chunks + i)
        waves = []
        for h in range(parts):
            spot = slice(h * peers, (h + 1) * peers)
            waves.append(restore(rec2[i, spot], sc_rec2[i, spot]).reshape(step, LANES))
        potential = right_table(jnp.concatenate(waves, axis=1), bwd_ref)
        high, low = split(
            jnp.concatenate([potential * chosen[1 - c, at, :].astype(F32) for c in range(2)], axis=0)
        )
        if i < chunks - 1:
            term = dot(turned_hots[i], high) + dot(turned_hots[i], low)
            acc[...] = term if i == 0 else acc[...] + term
            continue
        some = norb_rows // 4
        group = peers // 4
        for n in range(4):
            b = lax.rem(o // group + n + 1, 4)
            here = pl.ds(pl.multiple_of(b * some, some), some)
            hot = turned_hots[i, here, :]
            total = -(acc[here, :] + dot(hot, high) + dot(hot, low))
            coded, scale = quantize(total.reshape(group, orb_dev * rows, width))
            snd3[pl.ds(b * group, group)] = coded
            sc_snd3[pl.ds(b * group, group)] = scale

            def deliver(j, c):
                p = b * group + j

                @pl.when(p != o)
                def _():
                    remote(sc_snd3.at[p], sc_rec3.at[o], last, (p, f)).start()
                    remote(snd3.at[p], rec3.at[o], last + 1, (p, f)).start()

                @pl.when(p == o)
                def _():
                    pltpu.make_async_copy(sc_snd3.at[p], sc_rec3.at[o], recv_sem.at[last]).start()
                    pltpu.make_async_copy(snd3.at[p], rec3.at[o], recv_sem.at[last + 1]).start()

                return c

            lax.fori_loop(0, group, deliver, 0)

    left(names, 0)
    left(held, 1)
    gone = whole.at[pl.ds(0, parts - 1)]
    pltpu.make_async_copy(gone, gone, send_sem.at[2]).wait()
    for i in range(chunks):
        left(sc_snd1.at[i], 3 + i)
        left(snd1.at[i], 3 + chunks + i)
        left(sc_snd2.at[i], 3 + 2 * chunks + i)
        left(snd2.at[i], 3 + 3 * chunks + i)
    arrived(sc_rec3, last)
    arrived(rec3, last + 1)
    coded_ref[...] = rec3[...]
    rate_ref[...] = sc_rec3[...]
    left(sc_snd3, last)
    left(snd3, last + 1)


def unpack(rows, coded_ref, rate_ref, out_ref, done, sems):
    count, block, width = coded_ref.shape
    group = count // 4
    copies = []
    for n in range(4):
        for p in range(n * group, (n + 1) * group):
            values = restore(coded_ref[p : p + 1], rate_ref[p : p + 1])
            done[:, p * rows : (p + 1) * rows, :] = values.reshape(block // rows, rows, width)
        at = slice(n * group * rows, (n + 1) * group * rows)
        copy = pltpu.make_async_copy(done.at[:, at, :], out_ref.at[:, at, :], sems.at[n])
        copy.start()
        copies.append(copy)
    for copy in copies:
        copy.wait()


def tables_of(array):
    exact = jnp.asarray(array, F32)
    high = lax.reduce_precision(exact, 8, 7)
    return jnp.stack([high.astype(BF16), (exact - high).astype(BF16)])


def fused_device(orbitals, kernel, partner_owner, partner_local):
    peers = lax.axis_size("orb")
    parts = lax.axis_size("fft")
    orb_dev, rows_x, width = orbitals.shape
    task_dev = partner_local.shape[0]
    rows = rows_x // peers
    full_x = rows_x * parts
    everyone = peers * parts
    block = orb_dev * rows
    half = width // 2
    per = half // parts

    forward, backward = packed_tables(width)
    order = np.concatenate(
        [np.concatenate([np.arange(h * per, (h + 1) * per), half + np.arange(h * per, (h + 1) * per)]) for h in range(parts)]
    )
    angle = angles(full_x)
    both = np.concatenate([np.cos(angle), np.sin(angle)], axis=0)
    vmem = pl.BlockSpec(memory_space=pltpu.VMEM)
    hbm = pl.BlockSpec(memory_space=pltpu.HBM)
    pack = 2
    chunks = task_dev // pack
    deep = pack * rows
    ways = [
        pltpu.VMEM((chunks, everyone, deep, LANES), jnp.int16), pltpu.VMEM((chunks, everyone, deep, LANES), jnp.int16),
        pltpu.VMEM((chunks, everyone, 1, LANES), F32), pltpu.VMEM((chunks, everyone, 1, LANES), F32),
    ]
    rows_all = task_dev * peers * rows
    orb_rows = peers * block
    sems = 5 + 4 * chunks
    coded, rate = pl.pallas_call(
        functools.partial(fused, peers, parts, rows, orb_dev, task_dev),
        out_shape=(
            jax.ShapeDtypeStruct((peers, block, width), jnp.int16),
            jax.ShapeDtypeStruct((peers, 1, LANES), F32),
        ),
        in_specs=[hbm] + [pl.BlockSpec(memory_space=pltpu.SMEM)] * 2 + [hbm] * 4,
        out_specs=(vmem, vmem),
        scratch_shapes=[
            pltpu.VMEM((task_dev, LANES), F32),
            pltpu.VMEM((2, width, width), BF16), pltpu.VMEM((2, width, width), BF16),
            pltpu.VMEM((2, 2 * full_x, full_x), BF16),
            pltpu.VMEM((peers, orb_dev, rows, width), BF16),
            pltpu.VMEM((peers, task_dev, LANES), F32),
            pltpu.VMEM((parts,) + kernel.shape, F32),
            pltpu.VMEM((2, rows_all, width), BF16),
            *ways, *ways,
            pltpu.VMEM((2, rows_all, orb_rows), BF16),
            pltpu.VMEM((chunks, orb_rows, 2 * rows_all // chunks), BF16),
            pltpu.VMEM((orb_rows, width), F32),
            pltpu.VMEM((peers, block, width), jnp.int16), pltpu.VMEM((peers, block, width), jnp.int16),
            pltpu.VMEM((peers, 1, LANES), F32), pltpu.VMEM((peers, 1, LANES), F32),
            pltpu.SemaphoreType.DMA((sems,)),
            pltpu.SemaphoreType.DMA((sems,)),
            pltpu.SemaphoreType.DMA((3,)),
        ],
        compiler_params=pltpu.CompilerParams(
            collective_id=0, has_side_effects=True, vmem_limit_bytes=48 * 1024 * 1024
        ),
    )(
        orbitals, partner_owner.transpose(1, 2, 0), partner_local.T, kernel,
        tables_of(forward[:, order]), tables_of(backward[order]), tables_of(both),
    )
    return pl.pallas_call(
        functools.partial(unpack, rows),
        out_shape=jax.ShapeDtypeStruct((orb_dev, rows_x, width), F32),
        in_specs=[vmem, vmem],
        out_specs=hbm,
        scratch_shapes=[pltpu.VMEM((orb_dev, rows_x, width), F32), pltpu.SemaphoreType.DMA((4,))],
        compiler_params=pltpu.CompilerParams(vmem_limit_bytes=16 * 1024 * 1024),
    )(coded, rate)


def on_device(orbitals, kernel, partner_owner, partner_local):
    peers = lax.axis_size("orb")
    parts = lax.axis_size("fft")
    orb_dev, rows_x, width = orbitals.shape
    fits = rows_x == 8 * peers and width == LANES * parts and peers % 4 == 0
    fits = fits and orb_dev == 8 and partner_local.shape[0] == 8 and orb_dev * peers <= LANES
    step = fused_device if fits else plain_device
    return step(orbitals, kernel, partner_owner, partner_local)


def solution(mesh):
    in_specs = (P("orb", "fft", None), P("fft", None), P("orb", None, None), P("orb", None))
    out_specs = P("orb", "fft", None)
    return jax.shard_map(
        on_device, mesh=mesh, in_specs=in_specs, out_specs=out_specs, check_vma=False
    )
```

```python
import functools
import math

import jax
import jax.numpy as jnp
import numpy as np
from jax import lax
from jax.experimental import pallas as pl
from jax.experimental.pallas import tpu as pltpu
from jax.sharding import PartitionSpec as P

LEVELS = 32767.0
STEPS = 128.0
LANES = 128
VMEM_GRANT = 66469888


def angles(length):
    series = np.arange(length)
    return (series[:, None] * series[None, :] % length) * (2.0 * math.pi / length)


def packed_tables(length):
    half = length // 2
    angle = angles(length)[:, :half]
    sine = np.sin(angle)
    sine[:, 0] = np.cos(math.pi * np.arange(length))
    forward = np.concatenate([np.cos(angle), sine], axis=1)
    gain = np.full((2 * half,), 2.0)
    gain[0] = gain[half] = 1.0
    backward = (forward * gain).T
    return forward.astype(np.float32), backward.astype(np.float32)


def product(form, left, right):
    return jnp.einsum(form, left, right, precision=lax.Precision.HIGH, preferred_element_type=jnp.float32)


def weights(kernel):
    half = kernel.shape[0] // 2
    mirror = jnp.roll(jnp.flip(kernel, (0, 1)), 1, (0, 1))
    even = (0.5 * (kernel + mirror)).T
    plus = even[:, :half]
    minus = jnp.concatenate([even[:, half : half + 1], even[:, 1:half]], axis=1)
    return plus, minus


def convolve(density, kernel):
    full_x, width_y = density.shape[1:]
    half = width_y // 2
    forward, backward = packed_tables(width_y)
    angle = angles(full_x)
    both = np.concatenate([np.cos(angle), np.sin(angle)], axis=0).astype(np.float32)
    plus, minus = weights(kernel)
    scale = 1.0 / (full_x * width_y)
    weight = jnp.concatenate([plus, minus], axis=1) * scale
    spread = product("txy,yk->txk", density, forward)
    mixed = product("qx,txk->tqk", both, spread)
    cos_part = mixed[:, :full_x] * weight
    sin_part = mixed[:, full_x:] * weight
    first = cos_part[:, :, :half] - sin_part[:, :, half:]
    second = sin_part[:, :, :half] + cos_part[:, :, half:]
    back = product("qx,txk->tqk", both, jnp.concatenate([first, second], axis=2))
    cos_part = back[:, :full_x]
    sin_part = back[:, full_x:]
    real = cos_part[:, :, :half] + sin_part[:, :, half:]
    imag = cos_part[:, :, half:] - sin_part[:, :, :half]
    return product("txk,ky->txy", jnp.concatenate([real, imag], axis=2), backward)


def encode(values, run):
    rows, width = values.shape
    runs = values.reshape(rows, width // run, run)
    peak = jnp.maximum(jnp.max(jnp.abs(runs), axis=2), 1e-30)
    level = jnp.ceil(jnp.log2(peak) * STEPS + 0.01)
    rate = jnp.exp2(level / STEPS)
    coded = jnp.round(runs * (LEVELS / rate)[:, :, None]).reshape(rows, width)
    extra = jnp.pad(level, ((0, 0), (0, LANES - width // run)))
    return jnp.concatenate([coded, extra], axis=1).astype(jnp.int16)


def decode(coded, run):
    rows = coded.shape[0]
    width = coded.shape[1] - LANES
    level = coded[:, width : width + width // run].astype(jnp.float32)
    rate = jnp.exp2(level / STEPS) / LEVELS
    runs = coded[:, :width].astype(jnp.float32).reshape(rows, width // run, run)
    return (runs * rate[:, :, None]).reshape(rows, width)


def plain_device(orbitals, kernel, partner_owner, partner_local):
    peers = lax.axis_size("orb")
    parts = lax.axis_size("fft")
    orb_dev, rows_x, width_y = orbitals.shape
    tasks_dev = partner_local.shape[0]
    tasks = tasks_dev * peers
    norb = orb_dev * peers
    full_x = rows_x * parts
    chunk = rows_x * width_y // peers
    run = min(width_y, chunk)
    own = tasks // (peers * parts)

    whole = lax.all_to_all(
        jnp.broadcast_to(kernel[None], (parts,) + kernel.shape), "fft", 0, 0, tiled=True
    ).reshape(parts * kernel.shape[0], kernel.shape[1])
    named = partner_owner[:, :, 0] * orb_dev + partner_local
    named = jnp.broadcast_to(named[None], (peers, tasks_dev, 2))
    pair_ids = lax.all_to_all(named, "orb", 0, 0, tiled=True).reshape(tasks, 2)
    held = lax.all_to_all(
        orbitals.reshape(orb_dev, peers, chunk).transpose(1, 0, 2), "orb", 0, 0, tiled=True
    ).reshape(norb, chunk)

    pick = (pair_ids.T.reshape(2 * tasks, 1) == jnp.arange(norb, dtype=jnp.int32)[None, :]).astype(jnp.bfloat16)
    chosen = jnp.dot(pick, held, preferred_element_type=jnp.float32)
    first, second = chosen[:tasks], chosen[tasks:]
    density = first * second

    sent = encode(density, run).reshape(parts, peers, own, chunk + LANES)
    got = lax.all_to_all(sent.reshape(parts * peers * own, chunk + LANES), ("fft", "orb"), 0, 0, tiled=True)
    grid = decode(got, run).reshape(parts * peers, own, chunk)
    grid = grid.transpose(1, 0, 2).reshape(own, full_x, width_y)
    potential = convolve(grid, whole)
    potential = potential.reshape(own, parts * peers, chunk).transpose(1, 0, 2)
    sent = encode(potential.reshape(parts * peers * own, chunk), run)
    got = lax.all_to_all(sent, ("fft", "orb"), 0, 0, tiled=True)
    potential = decode(got, run)

    terms = jnp.concatenate([potential * second, potential * first], axis=0)
    high = lax.reduce_precision(terms, 8, 7)
    low = (terms - high).astype(jnp.bfloat16)
    high = high.astype(jnp.bfloat16)
    total = jnp.einsum(
        "to,tc->oc",
        jnp.concatenate([pick, pick], axis=0),
        jnp.concatenate([high, low], axis=0),
        preferred_element_type=jnp.float32,
    )
    sent = encode(-total, run)
    got = decode(lax.all_to_all(sent, "orb", 0, 0, tiled=True), run)
    return got.reshape(peers, orb_dev, chunk).transpose(1, 0, 2).reshape(orb_dev, rows_x, width_y)


F32 = jnp.float32
BF16 = jnp.bfloat16
MESH = pl.DeviceIdType.MESH


def split(values):
    high = values.astype(BF16)
    return high, (values - high.astype(F32)).astype(BF16)


def dot(left, right):
    return jnp.dot(left, right, preferred_element_type=F32)


def left_table(table, values):
    high, low = split(values)
    return dot(table[0], high) + dot(table[0], low) + dot(table[1], high)


def right_table(values, table):
    high, low = split(values)
    return dot(high, table[0]) + dot(low, table[0]) + dot(high, table[1])


def iota(shape, axis):
    return lax.broadcasted_iota(jnp.int32, shape, axis)


def quantize(values, first_row=0):
    count, rows, _ = values.shape
    peak = jnp.maximum(jnp.max(jnp.abs(values), axis=2, keepdims=True), 1e-30)
    coded = jnp.round(values * (LEVELS / peak)).astype(jnp.int32).astype(jnp.int16)
    shape = (count, rows, LANES)
    spot = iota(shape, 2) == iota(shape, 1) + first_row
    scale = jnp.sum(jnp.where(spot, peak * (1.0 / LEVELS), 0.0), axis=1, keepdims=True)
    return coded, scale


def restore(coded, scale, first_row=0):
    count, rows, _ = coded.shape
    shape = (count, rows, LANES)
    spot = iota(shape, 2) == iota(shape, 1) + first_row
    rate = jnp.sum(jnp.where(spot, jnp.broadcast_to(scale, shape), 0.0), axis=2, keepdims=True)
    return coded.astype(jnp.int32).astype(F32) * rate


def half_roll(values):
    parts = [
        pltpu.roll(values[:, at : at + LANES], LANES // 2, 1) for at in range(0, values.shape[1], LANES)
    ]
    return jnp.concatenate(parts, axis=1)


def fused(
    peers, parts, rows, orb_dev, task_dev,
    orb_ref, owner_ref, local_ref, ker_ref, fwd_hbm, bwd_hbm, both_hbm, coded_ref, rate_ref,
    ids, fwd_ref, bwd_ref, both_ref, held, names, whole, chosen, snd1, rec1, sc_snd1, sc_rec1, snd2, rec2, sc_snd2, sc_rec2,
    hots, turned_hots, acc, snd3, rec3, sc_snd3, sc_rec3, send_sem, recv_sem, table_sem,
):
    o = lax.axis_index("orb")
    f = lax.axis_index("fft")
    everyone = peers * parts
    me = f * peers + o
    tasks = task_dev * peers
    width = orb_ref.shape[2]
    half = width // 2
    full_x = ker_ref.shape[1]
    deep = snd1.shape[2]
    chunks = snd1.shape[0]
    step = peers * deep
    total_rows = tasks * rows
    norb_rows = peers * orb_dev * rows
    pack = deep // rows

    fetches = [
        pltpu.make_async_copy(src, dst, table_sem.at[n])
        for n, (src, dst) in enumerate(((fwd_hbm, fwd_ref), (bwd_hbm, bwd_ref), (both_hbm, both_ref)))
    ]
    for fetch in fetches:
        fetch.start()
    table = jnp.zeros((task_dev, LANES), F32)
    for t in range(task_dev):
        for c in range(2):
            spot = (iota(table.shape, 0) == t) & (iota(table.shape, 1) == c)
            table = jnp.where(spot, (owner_ref[c, 0, t] * orb_dev + local_ref[c, t]).astype(F32), table)
    ids[...] = table

    barrier = pltpu.get_barrier_semaphore()

    def greet(i, c):
        p = lax.rem(me + i, everyone)
        pl.semaphore_signal(barrier, inc=1, device_id=(lax.rem(p, peers), p // peers), device_id_type=MESH)
        return c

    lax.fori_loop(1, everyone, greet, 0)
    pl.semaphore_wait(barrier, everyone - 1)

    def remote(src, dst, k, device):
        return pltpu.make_async_remote_copy(
            src_ref=src, dst_ref=dst, send_sem=send_sem.at[k], recv_sem=recv_sem.at[k],
            device_id=device, device_id_type=MESH,
        )

    def over_orb(piece, dst, k):
        def one(i, c):
            p = lax.rem(o + i, peers)
            remote(piece(p), dst.at[o], k, (p, f)).start()
            return c

        pltpu.make_async_copy(piece(o), dst.at[o], recv_sem.at[k]).start()
        lax.fori_loop(1, peers, one, 0)

    def over_all(i, scale, scale_to, src, dst, k):
        def one(j, c):
            p = lax.rem(me + j, everyone)
            device = (lax.rem(p, peers), p // peers)
            remote(scale.at[i, p], scale_to.at[i, me], k + i, device).start()
            remote(src.at[i, p], dst.at[i, me], k + chunks + i, device).start()
            return c

        pltpu.make_async_copy(scale.at[i, me], scale_to.at[i, me], recv_sem.at[k + i]).start()
        pltpu.make_async_copy(src.at[i, me], dst.at[i, me], recv_sem.at[k + chunks + i]).start()
        lax.fori_loop(1, everyone, one, 0)

    def arrived(dst, k):
        pltpu.make_async_copy(dst, dst, recv_sem.at[k]).wait()

    def left(dst, k):
        gone = dst.at[pl.ds(0, dst.shape[0] - 1)]
        pltpu.make_async_copy(gone, gone, send_sem.at[k]).wait()

    over_orb(lambda p: ids, names, 0)
    over_orb(lambda p: orb_ref.at[:, pl.ds(pl.multiple_of(p * rows, rows), rows), :], held, 1)

    def halves(i, c):
        p = lax.rem(f + i, parts)
        remote(ker_ref, whole.at[f], 2, (o, p)).start()
        return c

    pltpu.make_async_copy(ker_ref, whole.at[f], recv_sem.at[2]).start()
    lax.fori_loop(1, parts, halves, 0)

    def task_of(row):
        return row // deep % peers * task_dev + row // step * pack + row // rows % pack

    arrived(names, 0)
    named = names[...].reshape(tasks, LANES)
    grow = (task_of(iota((total_rows, tasks), 0)) == iota((total_rows, tasks), 1)).astype(F32).astype(BF16)
    down = dot(grow, named.astype(BF16)).astype(jnp.int32) * rows + iota((total_rows, LANES), 0) % rows
    spread = (task_of(iota((tasks, total_rows), 1)) == iota((tasks, total_rows), 0)).astype(F32).astype(BF16)
    across = dot(named.T[:8].astype(BF16), spread).astype(jnp.int32) * rows + iota((8, total_rows), 1) % rows
    for i in range(chunks):
        at = slice(i * step, (i + 1) * step)
        for c in range(2):
            hot = down[at, c : c + 1] == iota((step, norb_rows), 1)
            hots[c, at, :] = hot.astype(F32).astype(BF16)
            hot = across[c : c + 1, at] == iota((norb_rows, step), 0)
            turned_hots[i, :, c * step : (c + 1) * step] = hot.astype(F32).astype(BF16)

    arrived(whole, 2)
    per = half // parts
    turned = split(whole[...].reshape(width, full_x).T)
    lane = iota((width, LANES), 1)
    freq = f * per + lax.rem(lane, per)
    freq = jnp.where((lane >= per) & (freq == 0), half, freq)
    row = iota((width, LANES), 0)
    straight = (row == freq).astype(F32).astype(BF16)
    mirror = (row == lax.rem(width - freq, width)).astype(F32).astype(BF16)
    flip_shape = (full_x, full_x)
    flip = (iota(flip_shape, 1) == lax.rem(full_x - iota(flip_shape, 0), full_x)).astype(F32).astype(BF16)
    plain = dot(turned[0], straight) + dot(turned[1], straight)
    other = split(dot(turned[0], mirror) + dot(turned[1], mirror))
    weight = (plain + dot(flip, other[0]) + dot(flip, other[1])) * (0.5 / (full_x * width))
    sign = jnp.where(iota((full_x, pack * LANES), 1) % LANES < per, 1.0, -1.0)
    weight = jnp.concatenate([weight] * pack, axis=1)
    signed = weight * sign

    for fetch in fetches:
        fetch.wait()
    arrived(held, 1)
    source = held[...].reshape(norb_rows, width)
    for i in range(chunks):
        at = slice(i * step, (i + 1) * step)
        pair = []
        for c in range(2):
            value = dot(hots[c, at, :], source)
            chosen[c, at, :] = value.astype(BF16)
            pair.append(value)
        waves = right_table(pair[0] * pair[1], fwd_ref)
        for h in range(parts):
            coded, scale = quantize(waves[:, h * LANES : (h + 1) * LANES].reshape(peers, deep, LANES))
            snd1[i, h * peers : (h + 1) * peers] = coded
            sc_snd1[i, h * peers : (h + 1) * peers] = scale
        over_all(i, sc_snd1, sc_rec1, snd1, rec1, 3)

    for i in range(chunks):
        arrived(sc_rec1.at[i], 3 + i)
        arrived(rec1.at[i], 3 + chunks + i)
        values = restore(rec1[i], sc_rec1[i])
        grid = jnp.concatenate(
            [values[:, t * rows : (t + 1) * rows].reshape(full_x, LANES) for t in range(pack)], axis=1
        )
        mixed = left_table(both_ref, grid)
        mixed = mixed[:full_x] * weight + half_roll(mixed[full_x:] * signed)
        mixed = left_table(both_ref, mixed)
        mixed = mixed[:full_x] + half_roll(mixed[full_x:]) * sign
        values = jnp.concatenate(
            [mixed[:, t * LANES : (t + 1) * LANES].reshape(everyone, rows, LANES) for t in range(pack)], axis=1
        )
        coded, scale = quantize(values)
        snd2[i] = coded
        sc_snd2[i] = scale
        over_all(i, sc_snd2, sc_rec2, snd2, rec2, 3 + 2 * chunks)

    last = 3 + 4 * chunks
    for i in range(chunks):
        at = slice(i * step, (i + 1) * step)
        arrived(sc_rec2.at[i], 3 + 2 * chunks + i)
        arrived(rec2.at[i], 3 + 3 * chunks + i)
        waves = []
        for h in range(parts):
            spot = slice(h * peers, (h + 1) * peers)
            waves.append(restore(rec2[i, spot], sc_rec2[i, spot]).reshape(step, LANES))
        potential = right_table(jnp.concatenate(waves, axis=1), bwd_ref)
        high, low = split(
            jnp.concatenate([potential * chosen[1 - c, at, :].astype(F32) for c in range(2)], axis=0)
        )
        if i < chunks - 1:
            term = dot(turned_hots[i], high) + dot(turned_hots[i], low)
            acc[...] = term if i == 0 else acc[...] + term
            continue
        some = norb_rows // 4
        group = peers // 4
        for n in range(4):
            b = lax.rem(o // group + n + 1, 4)
            here = pl.ds(pl.multiple_of(b * some, some), some)
            hot = turned_hots[i, here, :]
            total = -(acc[here, :] + dot(hot, high) + dot(hot, low))
            coded, scale = quantize(total.reshape(group, orb_dev * rows, width))
            snd3[pl.ds(b * group, group)] = coded
            sc_snd3[pl.ds(b * group, group)] = scale

            def deliver(j, c):
                p = b * group + j

                @pl.when(p != o)
                def _():
                    remote(sc_snd3.at[p], sc_rec3.at[o], last, (p, f)).start()
                    remote(snd3.at[p], rec3.at[o], last + 1, (p, f)).start()

                @pl.when(p == o)
                def _():
                    pltpu.make_async_copy(sc_snd3.at[p], sc_rec3.at[o], recv_sem.at[last]).start()
                    pltpu.make_async_copy(snd3.at[p], rec3.at[o], recv_sem.at[last + 1]).start()

                return c

            lax.fori_loop(0, group, deliver, 0)

    left(names, 0)
    left(held, 1)
    gone = whole.at[pl.ds(0, parts - 1)]
    pltpu.make_async_copy(gone, gone, send_sem.at[2]).wait()
    for i in range(chunks):
        left(sc_snd1.at[i], 3 + i)
        left(snd1.at[i], 3 + chunks + i)
        left(sc_snd2.at[i], 3 + 2 * chunks + i)
        left(snd2.at[i], 3 + 3 * chunks + i)
    arrived(sc_rec3, last)
    arrived(rec3, last + 1)
    coded_ref[...] = rec3[...]
    rate_ref[...] = sc_rec3[...]
    left(sc_snd3, last)
    left(snd3, last + 1)


def unpack(rows, coded_hbm, rate_hbm, out_ref, coded_ref, rate_ref, done, sems):
    count, block, width = coded_ref.shape
    group = count // 4
    fetches = [pltpu.make_async_copy(rate_hbm, rate_ref, sems.at[4])]
    for n in range(4):
        at = pl.ds(n * group, group)
        fetches.append(pltpu.make_async_copy(coded_hbm.at[at], coded_ref.at[at], sems.at[5 + n]))
    for fetch in fetches:
        fetch.start()
    fetches[0].wait()
    copies = []
    for n in range(4):
        fetches[1 + n].wait()
        for p in range(n * group, (n + 1) * group):
            values = restore(coded_ref[p : p + 1], rate_ref[p : p + 1])
            done[:, p * rows : (p + 1) * rows, :] = values.reshape(block // rows, rows, width)
        at = slice(n * group * rows, (n + 1) * group * rows)
        copy = pltpu.make_async_copy(done.at[:, at, :], out_ref.at[:, at, :], sems.at[n])
        copy.start()
        copies.append(copy)
    for copy in copies:
        copy.wait()


def tables_of(array):
    exact = jnp.asarray(array, F32)
    high = lax.reduce_precision(exact, 8, 7)
    return jnp.stack([high.astype(BF16), (exact - high).astype(BF16)])


def fused_device(orbitals, kernel, partner_owner, partner_local):
    peers = lax.axis_size("orb")
    parts = lax.axis_size("fft")
    orb_dev, rows_x, width = orbitals.shape
    task_dev = partner_local.shape[0]
    rows = rows_x // peers
    full_x = rows_x * parts
    everyone = peers * parts
    block = orb_dev * rows
    half = width // 2
    per = half // parts

    forward, backward = packed_tables(width)
    order = np.concatenate(
        [np.concatenate([np.arange(h * per, (h + 1) * per), half + np.arange(h * per, (h + 1) * per)]) for h in range(parts)]
    )
    angle = angles(full_x)
    both = np.concatenate([np.cos(angle), np.sin(angle)], axis=0)
    vmem = pl.BlockSpec(memory_space=pltpu.VMEM)
    hbm = pl.BlockSpec(memory_space=pltpu.HBM)
    pack = 2
    chunks = task_dev // pack
    deep = pack * rows
    ways = [
        pltpu.VMEM((chunks, everyone, deep, LANES), jnp.int16), pltpu.VMEM((chunks, everyone, deep, LANES), jnp.int16),
        pltpu.VMEM((chunks, everyone, 1, LANES), F32), pltpu.VMEM((chunks, everyone, 1, LANES), F32),
    ]
    rows_all = task_dev * peers * rows
    orb_rows = peers * block
    sems = 5 + 4 * chunks
    coded, rate = pl.pallas_call(
        functools.partial(fused, peers, parts, rows, orb_dev, task_dev),
        out_shape=(
            jax.ShapeDtypeStruct((peers, block, width), jnp.int16),
            jax.ShapeDtypeStruct((peers, 1, LANES), F32),
        ),
        in_specs=[hbm] + [pl.BlockSpec(memory_space=pltpu.SMEM)] * 2 + [hbm] * 4,
        out_specs=(vmem, vmem),
        scratch_shapes=[
            pltpu.VMEM((task_dev, LANES), F32),
            pltpu.VMEM((2, width, width), BF16), pltpu.VMEM((2, width, width), BF16),
            pltpu.VMEM((2, 2 * full_x, full_x), BF16),
            pltpu.VMEM((peers, orb_dev, rows, width), BF16),
            pltpu.VMEM((peers, task_dev, LANES), F32),
            pltpu.VMEM((parts,) + kernel.shape, F32),
            pltpu.VMEM((2, rows_all, width), BF16),
            *ways, *ways,
            pltpu.VMEM((2, rows_all, orb_rows), BF16),
            pltpu.VMEM((chunks, orb_rows, 2 * rows_all // chunks), BF16),
            pltpu.VMEM((orb_rows, width), F32),
            pltpu.VMEM((peers, block, width), jnp.int16), pltpu.VMEM((peers, block, width), jnp.int16),
            pltpu.VMEM((peers, 1, LANES), F32), pltpu.VMEM((peers, 1, LANES), F32),
            pltpu.SemaphoreType.DMA((sems,)),
            pltpu.SemaphoreType.DMA((sems,)),
            pltpu.SemaphoreType.DMA((3,)),
        ],
        compiler_params=pltpu.CompilerParams(
            collective_id=0, has_side_effects=True, vmem_limit_bytes=VMEM_GRANT
        ),
    )(
        orbitals, partner_owner.transpose(1, 2, 0), partner_local.T, kernel,
        tables_of(forward[:, order]), tables_of(backward[order]), tables_of(both),
    )
    return pl.pallas_call(
        functools.partial(unpack, rows),
        out_shape=jax.ShapeDtypeStruct((orb_dev, rows_x, width), F32),
        in_specs=[hbm, hbm],
        out_specs=hbm,
        scratch_shapes=[
            pltpu.VMEM((peers, block, width), jnp.int16), pltpu.VMEM((peers, 1, LANES), F32),
            pltpu.VMEM((orb_dev, rows_x, width), F32), pltpu.SemaphoreType.DMA((9,)),
        ],
        compiler_params=pltpu.CompilerParams(vmem_limit_bytes=VMEM_GRANT),
    )(coded, rate)


def on_device(orbitals, kernel, partner_owner, partner_local):
    peers = lax.axis_size("orb")
    parts = lax.axis_size("fft")
    orb_dev, rows_x, width = orbitals.shape
    fits = rows_x == 8 * peers and width == LANES * parts and peers % 4 == 0
    fits = fits and orb_dev == 8 and partner_local.shape[0] == 8 and orb_dev * peers <= LANES
    step = fused_device if fits else plain_device
    return step(orbitals, kernel, partner_owner, partner_local)


def solution(mesh):
    in_specs = (P("orb", "fft", None), P("fft", None), P("orb", None, None), P("orb", None))
    out_specs = P("orb", "fft", None)
    return jax.shard_map(
        on_device, mesh=mesh, in_specs=in_specs, out_specs=out_specs, check_vma=False
    )
```

```python
import functools
import math

import jax
import jax.numpy as jnp
import numpy as np
from jax import lax
from jax.experimental import pallas as pl
from jax.experimental.pallas import tpu as pltpu
from jax.sharding import PartitionSpec as P

LEVELS = 32767.0
STEPS = 128.0
LANES = 128
VMEM_GRANT = 66469888


def angles(length):
    series = np.arange(length)
    return (series[:, None] * series[None, :] % length) * (2.0 * math.pi / length)


def packed_tables(length):
    half = length // 2
    angle = angles(length)[:, :half]
    sine = np.sin(angle)
    sine[:, 0] = np.cos(math.pi * np.arange(length))
    forward = np.concatenate([np.cos(angle), sine], axis=1)
    gain = np.full((2 * half,), 2.0)
    gain[0] = gain[half] = 1.0
    backward = (forward * gain).T
    return forward.astype(np.float32), backward.astype(np.float32)


def product(form, left, right):
    return jnp.einsum(form, left, right, precision=lax.Precision.HIGH, preferred_element_type=jnp.float32)


def weights(kernel):
    half = kernel.shape[0] // 2
    mirror = jnp.roll(jnp.flip(kernel, (0, 1)), 1, (0, 1))
    even = (0.5 * (kernel + mirror)).T
    plus = even[:, :half]
    minus = jnp.concatenate([even[:, half : half + 1], even[:, 1:half]], axis=1)
    return plus, minus


def convolve(density, kernel):
    full_x, width_y = density.shape[1:]
    half = width_y // 2
    forward, backward = packed_tables(width_y)
    angle = angles(full_x)
    both = np.concatenate([np.cos(angle), np.sin(angle)], axis=0).astype(np.float32)
    plus, minus = weights(kernel)
    scale = 1.0 / (full_x * width_y)
    weight = jnp.concatenate([plus, minus], axis=1) * scale
    spread = product("txy,yk->txk", density, forward)
    mixed = product("qx,txk->tqk", both, spread)
    cos_part = mixed[:, :full_x] * weight
    sin_part = mixed[:, full_x:] * weight
    first = cos_part[:, :, :half] - sin_part[:, :, half:]
    second = sin_part[:, :, :half] + cos_part[:, :, half:]
    back = product("qx,txk->tqk", both, jnp.concatenate([first, second], axis=2))
    cos_part = back[:, :full_x]
    sin_part = back[:, full_x:]
    real = cos_part[:, :, :half] + sin_part[:, :, half:]
    imag = cos_part[:, :, half:] - sin_part[:, :, :half]
    return product("txk,ky->txy", jnp.concatenate([real, imag], axis=2), backward)


def encode(values, run):
    rows, width = values.shape
    runs = values.reshape(rows, width // run, run)
    peak = jnp.maximum(jnp.max(jnp.abs(runs), axis=2), 1e-30)
    level = jnp.ceil(jnp.log2(peak) * STEPS + 0.01)
    rate = jnp.exp2(level / STEPS)
    coded = jnp.round(runs * (LEVELS / rate)[:, :, None]).reshape(rows, width)
    extra = jnp.pad(level, ((0, 0), (0, LANES - width // run)))
    return jnp.concatenate([coded, extra], axis=1).astype(jnp.int16)


def decode(coded, run):
    rows = coded.shape[0]
    width = coded.shape[1] - LANES
    level = coded[:, width : width + width // run].astype(jnp.float32)
    rate = jnp.exp2(level / STEPS) / LEVELS
    runs = coded[:, :width].astype(jnp.float32).reshape(rows, width // run, run)
    return (runs * rate[:, :, None]).reshape(rows, width)


def plain_device(orbitals, kernel, partner_owner, partner_local):
    peers = lax.axis_size("orb")
    parts = lax.axis_size("fft")
    orb_dev, rows_x, width_y = orbitals.shape
    tasks_dev = partner_local.shape[0]
    tasks = tasks_dev * peers
    norb = orb_dev * peers
    full_x = rows_x * parts
    chunk = rows_x * width_y // peers
    run = min(width_y, chunk)
    own = tasks // (peers * parts)

    whole = lax.all_to_all(
        jnp.broadcast_to(kernel[None], (parts,) + kernel.shape), "fft", 0, 0, tiled=True
    ).reshape(parts * kernel.shape[0], kernel.shape[1])
    named = partner_owner[:, :, 0] * orb_dev + partner_local
    named = jnp.broadcast_to(named[None], (peers, tasks_dev, 2))
    pair_ids = lax.all_to_all(named, "orb", 0, 0, tiled=True).reshape(tasks, 2)
    held = lax.all_to_all(
        orbitals.reshape(orb_dev, peers, chunk).transpose(1, 0, 2), "orb", 0, 0, tiled=True
    ).reshape(norb, chunk)

    pick = (pair_ids.T.reshape(2 * tasks, 1) == jnp.arange(norb, dtype=jnp.int32)[None, :]).astype(jnp.bfloat16)
    chosen = jnp.dot(pick, held, preferred_element_type=jnp.float32)
    first, second = chosen[:tasks], chosen[tasks:]
    density = first * second

    sent = encode(density, run).reshape(parts, peers, own, chunk + LANES)
    got = lax.all_to_all(sent.reshape(parts * peers * own, chunk + LANES), ("fft", "orb"), 0, 0, tiled=True)
    grid = decode(got, run).reshape(parts * peers, own, chunk)
    grid = grid.transpose(1, 0, 2).reshape(own, full_x, width_y)
    potential = convolve(grid, whole)
    potential = potential.reshape(own, parts * peers, chunk).transpose(1, 0, 2)
    sent = encode(potential.reshape(parts * peers * own, chunk), run)
    got = lax.all_to_all(sent, ("fft", "orb"), 0, 0, tiled=True)
    potential = decode(got, run)

    terms = jnp.concatenate([potential * second, potential * first], axis=0)
    high = lax.reduce_precision(terms, 8, 7)
    low = (terms - high).astype(jnp.bfloat16)
    high = high.astype(jnp.bfloat16)
    total = jnp.einsum(
        "to,tc->oc",
        jnp.concatenate([pick, pick], axis=0),
        jnp.concatenate([high, low], axis=0),
        preferred_element_type=jnp.float32,
    )
    sent = encode(-total, run)
    got = decode(lax.all_to_all(sent, "orb", 0, 0, tiled=True), run)
    return got.reshape(peers, orb_dev, chunk).transpose(1, 0, 2).reshape(orb_dev, rows_x, width_y)


F32 = jnp.float32
BF16 = jnp.bfloat16
MESH = pl.DeviceIdType.MESH


def split(values):
    high = values.astype(BF16)
    return high, (values - high.astype(F32)).astype(BF16)


def dot(left, right):
    return jnp.dot(left, right, preferred_element_type=F32)


def left_table(table, values):
    high, low = split(values)
    return dot(table[0], high) + dot(table[0], low) + dot(table[1], high)


def right_table(values, table):
    high, low = split(values)
    return dot(high, table[0]) + dot(low, table[0]) + dot(high, table[1])


def iota(shape, axis):
    return lax.broadcasted_iota(jnp.int32, shape, axis)


def quantize(values, first_row=0):
    count, rows, _ = values.shape
    peak = jnp.maximum(jnp.max(jnp.abs(values), axis=2, keepdims=True), 1e-30)
    coded = jnp.round(values * (LEVELS / peak)).astype(jnp.int32).astype(jnp.int16)
    shape = (count, rows, LANES)
    spot = iota(shape, 2) == iota(shape, 1) + first_row
    scale = jnp.sum(jnp.where(spot, peak * (1.0 / LEVELS), 0.0), axis=1, keepdims=True)
    return coded, scale


def restore(coded, scale, first_row=0):
    count, rows, _ = coded.shape
    shape = (count, rows, LANES)
    spot = iota(shape, 2) == iota(shape, 1) + first_row
    rate = jnp.sum(jnp.where(spot, jnp.broadcast_to(scale, shape), 0.0), axis=2, keepdims=True)
    return coded.astype(jnp.int32).astype(F32) * rate


def half_roll(values):
    parts = [
        pltpu.roll(values[:, at : at + LANES], LANES // 2, 1) for at in range(0, values.shape[1], LANES)
    ]
    return jnp.concatenate(parts, axis=1)


def fused(
    peers, parts, rows, orb_dev, task_dev,
    orb_ref, owner_ref, local_ref, ker_ref, fwd_hbm, bwd_hbm, both_hbm, coded_ref, rate_ref,
    ids, fwd_ref, bwd_ref, both_ref, held, names, whole, chosen, snd1, rec1, sc_snd1, sc_rec1, snd2, rec2, sc_snd2, sc_rec2,
    hots, turned_hots, acc, snd3, rec3, sc_snd3, sc_rec3, send_sem, recv_sem, table_sem,
):
    o = lax.axis_index("orb")
    f = lax.axis_index("fft")
    everyone = peers * parts
    me = f * peers + o
    turn = jnp.where(2 * o < peers, peers - 1, 1)
    tasks = task_dev * peers
    width = orb_ref.shape[2]
    half = width // 2
    full_x = ker_ref.shape[1]
    deep = snd1.shape[2]
    chunks = snd1.shape[0]
    step = peers * deep
    total_rows = tasks * rows
    norb_rows = peers * orb_dev * rows
    pack = deep // rows

    fetches = [
        pltpu.make_async_copy(src, dst, table_sem.at[n])
        for n, (src, dst) in enumerate(((fwd_hbm, fwd_ref), (bwd_hbm, bwd_ref), (both_hbm, both_ref)))
    ]
    for fetch in fetches:
        fetch.start()
    table = jnp.zeros((task_dev, LANES), F32)
    for t in range(task_dev):
        for c in range(2):
            spot = (iota(table.shape, 0) == t) & (iota(table.shape, 1) == c)
            table = jnp.where(spot, (owner_ref[c, 0, t] * orb_dev + local_ref[c, t]).astype(F32), table)
    ids[...] = table

    barrier = pltpu.get_barrier_semaphore()

    def greet(i, c):
        p = lax.rem(me + i, everyone)
        pl.semaphore_signal(barrier, inc=1, device_id=(lax.rem(p, peers), p // peers), device_id_type=MESH)
        return c

    lax.fori_loop(1, everyone, greet, 0)
    pl.semaphore_wait(barrier, everyone - 1)

    def remote(src, dst, k, device):
        return pltpu.make_async_remote_copy(
            src_ref=src, dst_ref=dst, send_sem=send_sem.at[k], recv_sem=recv_sem.at[k],
            device_id=device, device_id_type=MESH,
        )

    def over_orb(piece, dst, k):
        def one(i, c):
            p = lax.rem(o + turn * i, peers)
            remote(piece(p), dst.at[o], k, (p, f)).start()
            return c

        pltpu.make_async_copy(piece(o), dst.at[o], recv_sem.at[k]).start()
        lax.fori_loop(1, peers, one, 0)

    def over_all(i, scale, scale_to, src, dst, k):
        def one(j, c):
            device = (lax.rem(o + turn * (j // parts), peers), lax.rem(f + j, parts))
            p = device[1] * peers + device[0]
            remote(scale.at[i, p], scale_to.at[i, me], k + i, device).start()
            remote(src.at[i, p], dst.at[i, me], k + chunks + i, device).start()
            return c

        pltpu.make_async_copy(scale.at[i, me], scale_to.at[i, me], recv_sem.at[k + i]).start()
        pltpu.make_async_copy(src.at[i, me], dst.at[i, me], recv_sem.at[k + chunks + i]).start()
        lax.fori_loop(1, everyone, one, 0)

    def arrived(dst, k):
        pltpu.make_async_copy(dst, dst, recv_sem.at[k]).wait()

    def left(dst, k):
        gone = dst.at[pl.ds(0, dst.shape[0] - 1)]
        pltpu.make_async_copy(gone, gone, send_sem.at[k]).wait()

    over_orb(lambda p: ids, names, 0)
    over_orb(lambda p: orb_ref.at[:, pl.ds(pl.multiple_of(p * rows, rows), rows), :], held, 1)

    def halves(i, c):
        p = lax.rem(f + i, parts)
        remote(ker_ref, whole.at[f], 2, (o, p)).start()
        return c

    pltpu.make_async_copy(ker_ref, whole.at[f], recv_sem.at[2]).start()
    lax.fori_loop(1, parts, halves, 0)

    def task_of(row):
        return row // deep % peers * task_dev + row // step * pack + row // rows % pack

    arrived(names, 0)
    named = names[...].reshape(tasks, LANES)
    grow = (task_of(iota((total_rows, tasks), 0)) == iota((total_rows, tasks), 1)).astype(F32).astype(BF16)
    down = dot(grow, named.astype(BF16)).astype(jnp.int32) * rows + iota((total_rows, LANES), 0) % rows
    spread = (task_of(iota((tasks, total_rows), 1)) == iota((tasks, total_rows), 0)).astype(F32).astype(BF16)
    across = dot(named.T[:8].astype(BF16), spread).astype(jnp.int32) * rows + iota((8, total_rows), 1) % rows
    for i in range(chunks):
        at = slice(i * step, (i + 1) * step)
        for c in range(2):
            hot = down[at, c : c + 1] == iota((step, norb_rows), 1)
            hots[c, at, :] = hot.astype(F32).astype(BF16)
            hot = across[c : c + 1, at] == iota((norb_rows, step), 0)
            turned_hots[i, :, c * step : (c + 1) * step] = hot.astype(F32).astype(BF16)

    arrived(whole, 2)
    per = half // parts
    turned = split(whole[...].reshape(width, full_x).T)
    lane = iota((width, LANES), 1)
    freq = f * per + lax.rem(lane, per)
    freq = jnp.where((lane >= per) & (freq == 0), half, freq)
    row = iota((width, LANES), 0)
    straight = (row == freq).astype(F32).astype(BF16)
    mirror = (row == lax.rem(width - freq, width)).astype(F32).astype(BF16)
    flip_shape = (full_x, full_x)
    flip = (iota(flip_shape, 1) == lax.rem(full_x - iota(flip_shape, 0), full_x)).astype(F32).astype(BF16)
    plain = dot(turned[0], straight) + dot(turned[1], straight)
    other = split(dot(turned[0], mirror) + dot(turned[1], mirror))
    weight = (plain + dot(flip, other[0]) + dot(flip, other[1])) * (0.5 / (full_x * width))
    sign = jnp.where(iota((full_x, pack * LANES), 1) % LANES < per, 1.0, -1.0)
    weight = jnp.concatenate([weight] * pack, axis=1)
    signed = weight * sign

    for fetch in fetches:
        fetch.wait()
    arrived(held, 1)
    source = held[...].reshape(norb_rows, width)
    for i in range(chunks):
        at = slice(i * step, (i + 1) * step)
        pair = []
        for c in range(2):
            value = dot(hots[c, at, :], source)
            chosen[c, at, :] = value.astype(BF16)
            pair.append(value)
        waves = right_table(pair[0] * pair[1], fwd_ref)
        for h in range(parts):
            coded, scale = quantize(waves[:, h * LANES : (h + 1) * LANES].reshape(peers, deep, LANES))
            snd1[i, h * peers : (h + 1) * peers] = coded
            sc_snd1[i, h * peers : (h + 1) * peers] = scale
        over_all(i, sc_snd1, sc_rec1, snd1, rec1, 3)

    for i in range(chunks):
        arrived(sc_rec1.at[i], 3 + i)
        arrived(rec1.at[i], 3 + chunks + i)
        values = restore(rec1[i], sc_rec1[i])
        grid = jnp.concatenate(
            [values[:, t * rows : (t + 1) * rows].reshape(full_x, LANES) for t in range(pack)], axis=1
        )
        mixed = left_table(both_ref, grid)
        mixed = mixed[:full_x] * weight + half_roll(mixed[full_x:] * signed)
        mixed = left_table(both_ref, mixed)
        mixed = mixed[:full_x] + half_roll(mixed[full_x:]) * sign
        values = jnp.concatenate(
            [mixed[:, t * LANES : (t + 1) * LANES].reshape(everyone, rows, LANES) for t in range(pack)], axis=1
        )
        coded, scale = quantize(values)
        snd2[i] = coded
        sc_snd2[i] = scale
        over_all(i, sc_snd2, sc_rec2, snd2, rec2, 3 + 2 * chunks)

    last = 3 + 4 * chunks
    for i in range(chunks):
        at = slice(i * step, (i + 1) * step)
        arrived(sc_rec2.at[i], 3 + 2 * chunks + i)
        arrived(rec2.at[i], 3 + 3 * chunks + i)
        waves = []
        for h in range(parts):
            spot = slice(h * peers, (h + 1) * peers)
            waves.append(restore(rec2[i, spot], sc_rec2[i, spot]).reshape(step, LANES))
        potential = right_table(jnp.concatenate(waves, axis=1), bwd_ref)
        high, low = split(
            jnp.concatenate([potential * chosen[1 - c, at, :].astype(F32) for c in range(2)], axis=0)
        )
        if i < chunks - 1:
            term = dot(turned_hots[i], high) + dot(turned_hots[i], low)
            acc[...] = term if i == 0 else acc[...] + term
            continue
        some = norb_rows // 4
        group = peers // 4
        for n in range(4):
            b = lax.rem(o // group + n + 1, 4)
            here = pl.ds(pl.multiple_of(b * some, some), some)
            hot = turned_hots[i, here, :]
            total = -(acc[here, :] + dot(hot, high) + dot(hot, low))
            coded, scale = quantize(total.reshape(group, orb_dev * rows, width))
            snd3[pl.ds(b * group, group)] = coded
            sc_snd3[pl.ds(b * group, group)] = scale

            def deliver(j, c):
                p = b * group + j

                @pl.when(p != o)
                def _():
                    remote(sc_snd3.at[p], sc_rec3.at[o], last, (p, f)).start()
                    remote(snd3.at[p], rec3.at[o], last + 1, (p, f)).start()

                @pl.when(p == o)
                def _():
                    pltpu.make_async_copy(sc_snd3.at[p], sc_rec3.at[o], recv_sem.at[last]).start()
                    pltpu.make_async_copy(snd3.at[p], rec3.at[o], recv_sem.at[last + 1]).start()

                return c

            lax.fori_loop(0, group, deliver, 0)

    left(names, 0)
    left(held, 1)
    gone = whole.at[pl.ds(0, parts - 1)]
    pltpu.make_async_copy(gone, gone, send_sem.at[2]).wait()
    for i in range(chunks):
        left(sc_snd1.at[i], 3 + i)
        left(snd1.at[i], 3 + chunks + i)
        left(sc_snd2.at[i], 3 + 2 * chunks + i)
        left(snd2.at[i], 3 + 3 * chunks + i)
    arrived(sc_rec3, last)
    arrived(rec3, last + 1)
    coded_ref[...] = rec3[...]
    rate_ref[...] = sc_rec3[...]
    left(sc_snd3, last)
    left(snd3, last + 1)


def unpack(rows, coded_hbm, rate_hbm, out_ref, coded_ref, rate_ref, done, sems):
    count, block, width = coded_ref.shape
    group = count // 4
    fetches = [pltpu.make_async_copy(rate_hbm, rate_ref, sems.at[4])]
    for n in range(4):
        at = pl.ds(n * group, group)
        fetches.append(pltpu.make_async_copy(coded_hbm.at[at], coded_ref.at[at], sems.at[5 + n]))
    for fetch in fetches:
        fetch.start()
    fetches[0].wait()
    copies = []
    for n in range(4):
        fetches[1 + n].wait()
        for p in range(n * group, (n + 1) * group):
            values = restore(coded_ref[p : p + 1], rate_ref[p : p + 1])
            done[:, p * rows : (p + 1) * rows, :] = values.reshape(block // rows, rows, width)
        at = slice(n * group * rows, (n + 1) * group * rows)
        copy = pltpu.make_async_copy(done.at[:, at, :], out_ref.at[:, at, :], sems.at[n])
        copy.start()
        copies.append(copy)
    for copy in copies:
        copy.wait()


def tables_of(array):
    exact = jnp.asarray(array, F32)
    high = lax.reduce_precision(exact, 8, 7)
    return jnp.stack([high.astype(BF16), (exact - high).astype(BF16)])


def fused_device(orbitals, kernel, partner_owner, partner_local):
    peers = lax.axis_size("orb")
    parts = lax.axis_size("fft")
    orb_dev, rows_x, width = orbitals.shape
    task_dev = partner_local.shape[0]
    rows = rows_x // peers
    full_x = rows_x * parts
    everyone = peers * parts
    block = orb_dev * rows
    half = width // 2
    per = half // parts

    forward, backward = packed_tables(width)
    order = np.concatenate(
        [np.concatenate([np.arange(h * per, (h + 1) * per), half + np.arange(h * per, (h + 1) * per)]) for h in range(parts)]
    )
    angle = angles(full_x)
    both = np.concatenate([np.cos(angle), np.sin(angle)], axis=0)
    vmem = pl.BlockSpec(memory_space=pltpu.VMEM)
    hbm = pl.BlockSpec(memory_space=pltpu.HBM)
    pack = 2
    chunks = task_dev // pack
    deep = pack * rows
    ways = [
        pltpu.VMEM((chunks, everyone, deep, LANES), jnp.int16), pltpu.VMEM((chunks, everyone, deep, LANES), jnp.int16),
        pltpu.VMEM((chunks, everyone, 1, LANES), F32), pltpu.VMEM((chunks, everyone, 1, LANES), F32),
    ]
    rows_all = task_dev * peers * rows
    orb_rows = peers * block
    sems = 5 + 4 * chunks
    coded, rate = pl.pallas_call(
        functools.partial(fused, peers, parts, rows, orb_dev, task_dev),
        out_shape=(
            jax.ShapeDtypeStruct((peers, block, width), jnp.int16),
            jax.ShapeDtypeStruct((peers, 1, LANES), F32),
        ),
        in_specs=[hbm] + [pl.BlockSpec(memory_space=pltpu.SMEM)] * 2 + [hbm] * 4,
        out_specs=(vmem, vmem),
        scratch_shapes=[
            pltpu.VMEM((task_dev, LANES), F32),
            pltpu.VMEM((2, width, width), BF16), pltpu.VMEM((2, width, width), BF16),
            pltpu.VMEM((2, 2 * full_x, full_x), BF16),
            pltpu.VMEM((peers, orb_dev, rows, width), BF16),
            pltpu.VMEM((peers, task_dev, LANES), F32),
            pltpu.VMEM((parts,) + kernel.shape, F32),
            pltpu.VMEM((2, rows_all, width), BF16),
            *ways, *ways,
            pltpu.VMEM((2, rows_all, orb_rows), BF16),
            pltpu.VMEM((chunks, orb_rows, 2 * rows_all // chunks), BF16),
            pltpu.VMEM((orb_rows, width), F32),
            pltpu.VMEM((peers, block, width), jnp.int16), pltpu.VMEM((peers, block, width), jnp.int16),
            pltpu.VMEM((peers, 1, LANES), F32), pltpu.VMEM((peers, 1, LANES), F32),
            pltpu.SemaphoreType.DMA((sems,)),
            pltpu.SemaphoreType.DMA((sems,)),
            pltpu.SemaphoreType.DMA((3,)),
        ],
        compiler_params=pltpu.CompilerParams(
            collective_id=0, has_side_effects=True, vmem_limit_bytes=VMEM_GRANT
        ),
    )(
        orbitals, partner_owner.transpose(1, 2, 0), partner_local.T, kernel,
        tables_of(forward[:, order]), tables_of(backward[order]), tables_of(both),
    )
    return pl.pallas_call(
        functools.partial(unpack, rows),
        out_shape=jax.ShapeDtypeStruct((orb_dev, rows_x, width), F32),
        in_specs=[hbm, hbm],
        out_specs=hbm,
        scratch_shapes=[
            pltpu.VMEM((peers, block, width), jnp.int16), pltpu.VMEM((peers, 1, LANES), F32),
            pltpu.VMEM((orb_dev, rows_x, width), F32), pltpu.SemaphoreType.DMA((9,)),
        ],
        compiler_params=pltpu.CompilerParams(vmem_limit_bytes=VMEM_GRANT),
    )(coded, rate)


def on_device(orbitals, kernel, partner_owner, partner_local):
    peers = lax.axis_size("orb")
    parts = lax.axis_size("fft")
    orb_dev, rows_x, width = orbitals.shape
    fits = rows_x == 8 * peers and width == LANES * parts and peers % 4 == 0
    fits = fits and orb_dev == 8 and partner_local.shape[0] == 8 and orb_dev * peers <= LANES
    step = fused_device if fits else plain_device
    return step(orbitals, kernel, partner_owner, partner_local)


def solution(mesh):
    in_specs = (P("orb", "fft", None), P("fft", None), P("orb", None, None), P("orb", None))
    out_specs = P("orb", "fft", None)
    return jax.shard_map(
        on_device, mesh=mesh, in_specs=in_specs, out_specs=out_specs, check_vma=False
    )
```
